128 devices in a mesh: head: 8 (over x_hi, z), frame: 16 (over x_lo, y, core).
Axes of the slice: x: 4 (x_hi: 2, x_lo: 2; x = x_hi * 2 + x_lo), y: 4, z: 4, core: 2. Of those that a mesh axis runs over, the one named last changes fastest.
Arguments:
- queries: bfloat16 [16384, 2048], P(('frame', 'head')), may hold values from -6 to 6
- key_states: bfloat16 [16384, 2048], P(('frame', 'head')), may hold values from -6 to 6
- value_states: bfloat16 [16384, 2048], P(('frame', 'head')), may hold values from -6 to 6
- attn_out: bfloat16 [16384, 2048], P(('frame', 'head')), may hold values from -6 to 6
- grad_out: bfloat16 [16384, 2048], P(('frame', 'head')), may hold values from -192 to 192
- frame_order: int32 [16], replicated, may hold values from 0 to 15, each once
- block_live: int32 [16, 8, 8], replicated, may hold values from 0 to 1, as said below
Outputs:
- grad_queries: bfloat16 [16384, 2048], P('frame', 'head')
- grad_keys: bfloat16 [16384, 2048], P('frame', 'head')
- grad_values: bfloat16 [16384, 2048], P('frame', 'head')
The draws below stay inside these ranges and needn't reach their ends.
Inputs may be any that keep to these rules, and one draw needn't show every extreme that they name: `block_live`: every entry at distance 0 is 1; every entry at distances of 4 or more is 0.
All inputs are finite; a program needn't handle non-finite values.
Results may differ from the reference program's by a relative error of at most 0.0049.
Values may be sent and summed in bfloat16 or wider, within the bound.
A program may use at most 128 MiB of HBM per device.

```python
import jax
import jax.numpy as jnp
from jax import lax

HEADS = 16
HEAD_DIM = 128
REACH = 4
FRAMES = 16
FRAME_TOK = 1024
NBLK = 8
TOKENS = 16384


def draw_pair(key):
    width = HEADS * HEAD_DIM
    query_base = jnp.clip(jax.random.normal(jax.random.fold_in(key, 11), (TOKENS, width), jnp.float32), -6.0, 6.0)
    key_base = jnp.clip(jax.random.normal(jax.random.fold_in(key, 12), (TOKENS, width), jnp.float32), -6.0, 6.0)
    return (query_base, key_base)


def draw_queries(key, part):
    return draw_pair(key)[0].astype(jnp.bfloat16)


def draw_key_states(key, part):
    return draw_pair(key)[1].astype(jnp.bfloat16)


def draw_block_live(key, part):
    distance = jnp.arange(FRAMES, dtype=jnp.int32)
    shifts = jax.random.randint(jax.random.fold_in(key, 21), (FRAMES,), -1, 2).astype(jnp.int32)
    powers = jnp.left_shift(jnp.int32(1), jnp.arange(20, dtype=jnp.int32))
    levels = jnp.sum((distance[:, None] >= powers[None, :]).astype(jnp.int32), axis=1)
    band = jnp.maximum(jnp.right_shift(jnp.int32(NBLK), levels + 1), 1)
    band = jnp.where(distance < REACH, band, 0)
    rows = jnp.arange(NBLK, dtype=jnp.int32)
    offset = rows[None, :, None] - rows[None, None, :] - shifts[:, None, None]
    inside = jnp.abs(offset) < band[:, None, None]
    whole = (distance == 0)[:, None, None]
    return jnp.where(whole | inside, 1, 0).astype(jnp.int32)


def block_levels(key, extent, pieces, least, top_value):
    loudness, own = 1.0, jax.random.fold_in(key, 6)
    for position, blocks in pieces:
        draws = jnp.exp(jax.random.uniform(jax.random.fold_in(own, position), (blocks,), jnp.float32, least / len(pieces), top_value / len(pieces)))
        loudness = loudness * jnp.repeat(draws, extent[position] // blocks).reshape([-1 if axis == position else 1 for axis in range(len(extent))])
    return loudness


def centred(rng, extent, scale, bound, cuts=(), kind=jnp.bfloat16):
    drawn = scale * jax.random.normal(rng, extent, jnp.float32)
    if cuts:
        drawn = drawn * block_levels(rng, extent, cuts, -0.22, 0.18)
    return jnp.clip(drawn, -bound, bound).astype(kind)


def setup_inputs(seed: int = 0) -> dict:
    streams_of = jax.random.split(jax.random.key(seed), 8)
    queries = draw_queries(jax.random.fold_in(streams_of[7], 71), 0)
    key_states = draw_key_states(jax.random.fold_in(streams_of[7], 71), 0)
    value_states = centred(streams_of[2], (TOKENS, HEADS * HEAD_DIM), 1.0, 6.0, ((0, 128),))
    attn_out = centred(streams_of[3], (TOKENS, HEADS * HEAD_DIM), 1.0, 6.0, ((0, 128),))
    grad_out = centred(streams_of[4], (TOKENS, HEADS * HEAD_DIM), 32.0, 192.0, ((0, 128),))
    frame_order = jax.random.permutation(streams_of[5], FRAMES).astype(jnp.int32)
    block_live = draw_block_live(jax.random.fold_in(streams_of[7], 71), 0)
    return {"queries": queries, "key_states": key_states, "value_states": value_states, "attn_out": attn_out, "grad_out": grad_out, "frame_order": frame_order, "block_live": block_live}


def block_mask(block_live, frame_order, slot_query, slot_key):
    distance = jnp.abs(frame_order[slot_query] - frame_order[slot_key]).astype(jnp.int32)
    blocks = lax.dynamic_index_in_dim(block_live, distance, 0, keepdims=False)
    count = blocks.shape[0]
    width = FRAME_TOK // count
    spread = jnp.broadcast_to(blocks[:, None, :, None], (count, width, count, width))
    return jnp.any(blocks > 0), spread.reshape(FRAME_TOK, FRAME_TOK) > 0


def reference(queries, key_states, value_states, attn_out, grad_out, frame_order, block_live):
    scale = HEAD_DIM ** -0.5
    shape3 = (TOKENS, HEADS, HEAD_DIM)
    query_all = queries.reshape(shape3).astype(jnp.float32)
    key_all = key_states.reshape(shape3).astype(jnp.float32)
    value_all = value_states.reshape(shape3).astype(jnp.float32)
    grad_all = grad_out.reshape(shape3).astype(jnp.float32)
    delta_all = jnp.sum(grad_all * attn_out.reshape(shape3).astype(jnp.float32), axis=2)
    slots = jnp.arange(FRAMES, dtype=jnp.int32)

    def rows_of(array, slot):
        return lax.dynamic_slice_in_dim(array, (slot * FRAME_TOK).astype(jnp.int32), FRAME_TOK, 0)

    def totals_for(slot_query):
        query_blk = rows_of(query_all, slot_query)

        def over_keys(state, slot_key):
            live, mask = block_mask(block_live, frame_order, slot_query, slot_key)

            def update(current):
                peak, total = current
                scores = scale * jnp.einsum("qhd,khd->hqk", query_blk, rows_of(key_all, slot_key))
                new_peak = jnp.maximum(peak, jnp.max(jnp.where(mask, scores, -1e30), axis=2))
                fresh = jnp.sum(jnp.where(mask, jnp.exp(scores - new_peak[:, :, None]), 0.0), axis=2)
                return (new_peak, total * jnp.exp(peak - new_peak) + fresh)

            return lax.cond(live, update, lambda current: current, state), None

        start = (jnp.full((HEADS, FRAME_TOK), -1e30, jnp.float32), jnp.zeros((HEADS, FRAME_TOK), jnp.float32))
        peak, total = lax.scan(over_keys, start, slots)[0]
        return peak + jnp.log(total)

    log_all = lax.map(totals_for, slots)

    def frame_step(carry, slot_query):
        query_blk = rows_of(query_all, slot_query)
        grad_blk = rows_of(grad_all, slot_query)
        delta_blk = rows_of(delta_all, slot_query).T
        log_blk = lax.dynamic_index_in_dim(log_all, slot_query, 0, keepdims=False)

        def over_keys(state, slot_key):
            live, mask = block_mask(block_live, frame_order, slot_query, slot_key)

            def update(current):
                grad_query, grad_key_acc, grad_value_acc = current
                key_blk = rows_of(key_all, slot_key)
                value_blk = rows_of(value_all, slot_key)
                scores = scale * jnp.einsum("qhd,khd->hqk", query_blk, key_blk)
                probs = jnp.where(mask, jnp.exp(scores - log_blk[:, :, None]), 0.0)
                probs_low = probs.astype(jnp.bfloat16).astype(jnp.float32)
                grad_probs = jnp.einsum("qhd,khd->hqk", grad_blk, value_blk)
                grad_scores = (probs * (grad_probs - delta_blk[:, :, None])).astype(jnp.bfloat16).astype(jnp.float32)
                grad_query = grad_query + scale * jnp.einsum("hqk,khd->qhd", grad_scores, key_blk)
                begin = (slot_key * FRAME_TOK).astype(jnp.int32)
                key_term = scale * jnp.einsum("hqk,qhd->khd", grad_scores, query_blk)
                value_term = jnp.einsum("hqk,qhd->khd", probs_low, grad_blk)
                old_key = lax.dynamic_slice_in_dim(grad_key_acc, begin, FRAME_TOK, 0)
                old_value = lax.dynamic_slice_in_dim(grad_value_acc, begin, FRAME_TOK, 0)
                grad_key_acc = lax.dynamic_update_slice_in_dim(grad_key_acc, old_key + key_term, begin, 0)
                grad_value_acc = lax.dynamic_update_slice_in_dim(grad_value_acc, old_value + value_term, begin, 0)
                return (grad_query, grad_key_acc, grad_value_acc)

            return lax.cond(live, update, lambda current: current, state), None

        start = (jnp.zeros((FRAME_TOK, HEADS, HEAD_DIM), jnp.float32), carry[0], carry[1])
        grad_query, grad_key_acc, grad_value_acc = lax.scan(over_keys, start, slots)[0]
        return (grad_key_acc, grad_value_acc), grad_query

    start = (jnp.zeros(shape3, jnp.float32), jnp.zeros(shape3, jnp.float32))
    (grad_key_acc, grad_value_acc), grad_frames = lax.scan(frame_step, start, slots)
    width = HEADS * HEAD_DIM
    grad_queries = grad_frames.reshape(TOKENS, width).astype(jnp.bfloat16)
    grad_keys = grad_key_acc.reshape(TOKENS, width).astype(jnp.bfloat16)
    grad_values = grad_value_acc.reshape(TOKENS, width).astype(jnp.bfloat16)
    return (grad_queries, grad_keys, grad_values)
```

```python
import functools
import math

import jax
import jax.numpy as jnp
from jax import lax
from jax.experimental import pallas as pl
from jax.experimental.pallas import tpu as pltpu
from jax.sharding import PartitionSpec as P

HEADS = 16
HEAD_DIM = 128
SCALE = HEAD_DIM ** (-0.5)
SCALE2 = SCALE * math.log2(math.e)
NBLK = 8
BLK = 128
RING = 4
GROUP = 8
SLOTS = 48
FAR = 1e30
MESH = pl.DeviceIdType.MESH
ANY = pl.BlockSpec(memory_space=pl.ANY)
SMEM = pl.BlockSpec(memory_space=pltpu.SMEM)
VMEM = pl.BlockSpec(memory_space=pltpu.VMEM)
NT = (((1,), (1,)), ((), ()))
TN = (((0,), (0,)), ((), ()))


def place():
    head = lax.axis_index("head")
    frame = lax.axis_index("frame")
    half = frame // GROUP
    member = frame % GROUP
    return head, half, member


def gather_kernel(*refs):
    count = 5
    srcs = refs[:count]
    bufs = refs[count : 2 * count]
    send1, recv1, send2, recv2 = refs[2 * count :]
    head, half, member = place()
    plane = head * 2 + half
    ring, core = member // 2, member % 2
    up = ((ring + 1) % RING) * 2 + core
    down = ((ring + RING - 1) % RING) * 2 + core
    far = ((ring + 2) % RING) * 2 + core
    twin = ring * 2 + 1 - core

    def plane_peer(step):
        other = (plane + step) % HEADS
        return other, {"head": other // 2, "frame": (other % 2) * GROUP + member}

    def group_peer(slot):
        return {"head": head, "frame": half * GROUP + slot}

    barrier = pltpu.get_barrier_semaphore()
    for step in range(1, HEADS):
        pl.semaphore_signal(barrier, inc=1, device_id=plane_peer(step)[1], device_id_type=MESH)
    for slot in (up, down, twin):
        pl.semaphore_signal(barrier, inc=1, device_id=group_peer(slot), device_id_type=MESH)
    pl.semaphore_wait(barrier, HEADS - 1 + 3)

    def column(a, other):
        if a == count - 1:
            return srcs[a].at[other]
        return srcs[a].at[:, pl.ds(pl.multiple_of(other * HEAD_DIM, HEAD_DIM), HEAD_DIM)]

    for a in range(count):
        for step in range(1, HEADS):
            other, device = plane_peer(step)
            pltpu.make_async_remote_copy(
                src_ref=column(a, other),
                dst_ref=bufs[a].at[half, member, head],
                send_sem=send1.at[a],
                recv_sem=recv1.at[a],
                device_id=device,
                device_id_type=MESH,
            ).start()
        pltpu.make_async_copy(column(a, plane), bufs[a].at[half, member, head], recv1.at[a]).start()

    pending = []

    def push(a, number, part, slot, arrive):
        copy = pltpu.make_async_remote_copy(
            src_ref=part,
            dst_ref=part,
            send_sem=send2.at[a, number],
            recv_sem=recv2.at[a, arrive],
            device_id=group_peer(slot),
            device_id_type=MESH,
        )
        copy.start()
        pending.append(copy)

    def arrived(a, number, part):
        pltpu.make_async_copy(part, part, recv2.at[a, number]).wait()

    for a in range(count):
        own = bufs[a].at[:, member]
        pltpu.make_async_copy(own, own, recv1.at[a]).wait()
        push(a, 0, own, up, 0)
        push(a, 1, own, down, 1)
        push(a, 2, own, twin, 4)
    for a in range(count):
        part = bufs[a].at[:, down]
        arrived(a, 0, part)
        push(a, 3, bufs[a].at[0, down], up, 2)
        push(a, 4, part, twin, 5)
        part = bufs[a].at[:, up]
        arrived(a, 1, part)
        push(a, 5, bufs[a].at[1, up], down, 3)
        push(a, 6, part, twin, 6)
    for a in range(count):
        part = bufs[a].at[0, far]
        arrived(a, 2, part)
        push(a, 7, part, twin, 7)
        part = bufs[a].at[1, far]
        arrived(a, 3, part)
        push(a, 8, part, twin, 8)
    twin_up = ((ring + 1) % RING) * 2 + 1 - core
    twin_down = ((ring + RING - 1) % RING) * 2 + 1 - core
    twin_far = ((ring + 2) % RING) * 2 + 1 - core
    for a in range(count):
        arrived(a, 4, bufs[a].at[:, twin])
        arrived(a, 5, bufs[a].at[:, twin_down])
        arrived(a, 6, bufs[a].at[:, twin_up])
        arrived(a, 7, bufs[a].at[0, twin_far])
        arrived(a, 8, bufs[a].at[1, twin_far])
    for copy in pending:
        copy.wait_send()
    for a in range(count):
        if a == count - 1:
            sent = srcs[a].at[pl.ds(0, HEADS - 1)]
        else:
            sent = srcs[a].at[:, pl.ds(0, (HEADS - 1) * HEAD_DIM)]
        pltpu.make_async_copy(sent, sent, send1.at[a]).wait()


def gather_all(key, value, query, grad, delta):
    whole = jax.ShapeDtypeStruct((2, GROUP, NBLK, BLK, HEAD_DIM), jnp.bfloat16)
    small = jax.ShapeDtypeStruct((2, GROUP, NBLK, 1, BLK), jnp.float32)
    return pl.pallas_call(
        gather_kernel,
        out_shape=(whole, whole, whole, whole, small),
        in_specs=[ANY] * 5,
        out_specs=(ANY,) * 5,
        scratch_shapes=[
            pltpu.SemaphoreType.DMA((5,)),
            pltpu.SemaphoreType.DMA((5,)),
            pltpu.SemaphoreType.DMA((5, 9)),
            pltpu.SemaphoreType.DMA((5, 9)),
        ],
        compiler_params=pltpu.CompilerParams(collective_id=0, has_side_effects=True),
        name="gather_all",
    )(key, value, query, grad, delta)


def share_kernel(own_ref, all_ref, send, recv, local):
    head, half, member = place()

    def peer(step):
        return {"head": head, "frame": half * GROUP + (member + step) % GROUP}

    barrier = pltpu.get_barrier_semaphore()
    for step in range(1, GROUP):
        pl.semaphore_signal(barrier, inc=1, device_id=peer(step), device_id_type=MESH)
    pl.semaphore_wait(barrier, GROUP - 1)
    copies = []
    for step in range(1, GROUP):
        copy = pltpu.make_async_remote_copy(
            src_ref=own_ref,
            dst_ref=all_ref.at[:, member],
            send_sem=send.at[step],
            recv_sem=recv.at[step],
            device_id=peer(step),
            device_id_type=MESH,
        )
        copy.start()
        copies.append(copy)
    mine = pltpu.make_async_copy(own_ref, all_ref.at[:, member], local)
    mine.start()
    mine.wait()
    for copy in copies:
        copy.wait()


def share_totals(own):
    return pl.pallas_call(
        share_kernel,
        out_shape=jax.ShapeDtypeStruct((2, GROUP, NBLK, 1, BLK), jnp.float32),
        in_specs=[VMEM],
        out_specs=VMEM,
        scratch_shapes=[
            pltpu.SemaphoreType.DMA((GROUP,)),
            pltpu.SemaphoreType.DMA((GROUP,)),
            pltpu.SemaphoreType.DMA,
        ],
        compiler_params=pltpu.CompilerParams(collective_id=1, has_side_effects=True),
        name="share_totals",
    )(own)


def dot(a, b, dims=(((1,), (0,)), ((), ()))):
    return lax.dot_general(a, b, dims, preferred_element_type=jnp.float32)


def query_kernel(member_ref, trips_ref, count_ref, list_ref, q_ref, g_ref, d_ref, k_ref, v_ref, dq_ref, lse_ref,
                 peak, total, acc):
    wide = 256
    member = member_ref[0]
    for unit in range(2):
        first = (unit * GROUP + member) * NBLK
        key = k_ref[pl.ds(first, NBLK)].reshape(NBLK * BLK, HEAD_DIM)
        value = v_ref[pl.ds(first, NBLK)].reshape(NBLK * BLK, HEAD_DIM)
        for part in range(NBLK * BLK // wide):
            i = part * 2
            query = q_ref[unit, 0, i : i + 2].reshape(wide, HEAD_DIM)
            grad = g_ref[unit, 0, i : i + 2].reshape(wide, HEAD_DIM)
            delta = jnp.concatenate([d_ref[unit, 0, i], d_ref[unit, 0, i + 1]], axis=1)
            scores = dot(key, query, NT) * SCALE2
            top = jnp.max(scores, axis=0, keepdims=True)
            probs = jnp.exp2(scores - top)
            summed = jnp.sum(probs, axis=0, keepdims=True)
            terms = (probs * (dot(value, grad, NT) - delta)).astype(jnp.bfloat16)
            partial = dot(key, terms, TN)
            for s in range(2):
                lanes = slice(s * BLK, (s + 1) * BLK)
                peak[unit * NBLK + i + s] = top[:, lanes]
                total[unit * NBLK + i + s] = summed[:, lanes]
                acc[unit * NBLK + i + s] = partial[:, lanes]

    def step(turn, carry):
        for unit in range(2):
            for i in range(NBLK):
                row = unit * NBLK + i
                entry = list_ref[row, turn]
                bias = jnp.where(turn < count_ref[row], 0.0, -FAR)
                key = k_ref[entry]
                value = v_ref[entry]
                scores = dot(key, q_ref[unit, 0, i], NT) * SCALE2 + bias
                before = peak[row]
                top = jnp.maximum(before, jnp.max(scores, axis=0, keepdims=True))
                shrink = jnp.exp2(before - top)
                probs = jnp.exp2(scores - top)
                terms = (probs * (dot(value, g_ref[unit, 0, i], NT) - d_ref[unit, 0, i])).astype(jnp.bfloat16)
                peak[row] = top
                total[row] = total[row] * shrink + jnp.sum(probs, axis=0, keepdims=True)
                acc[row] = acc[row] * shrink + dot(key, terms, TN)
        return carry

    lax.fori_loop(0, trips_ref[0], step, 0)
    for unit in range(2):
        for i in range(NBLK):
            row = unit * NBLK + i
            lse_ref[unit, i] = peak[row] + jnp.log2(total[row])
            done = acc[row] * (SCALE / total[row])
            dq_ref[unit, i] = done.T.astype(jnp.bfloat16)


def key_kernel(member_ref, trips_ref, count_ref, list_ref, k_ref, v_ref, d_ref, lse_ref, q_ref, g_ref, dk_ref, dv_ref,
               key_acc, value_acc):
    wide = 256
    member = member_ref[0]
    for unit in range(2):
        first = (unit * GROUP + member) * NBLK
        query = q_ref[pl.ds(first, NBLK)].reshape(NBLK * BLK, HEAD_DIM)
        grad = g_ref[pl.ds(first, NBLK)].reshape(NBLK * BLK, HEAD_DIM)
        delta = jnp.concatenate([d_ref[first + i] for i in range(NBLK)], axis=1)
        lse = jnp.concatenate([lse_ref[first + i] for i in range(NBLK)], axis=1)
        for part in range(NBLK * BLK // wide):
            u = part * 2
            key = k_ref[unit, 0, u : u + 2].reshape(wide, HEAD_DIM)
            value = v_ref[unit, 0, u : u + 2].reshape(wide, HEAD_DIM)
            probs = jnp.exp2(dot(key, query, NT) * SCALE2 - lse)
            terms = (probs * (dot(value, grad, NT) - delta)).astype(jnp.bfloat16)
            value_part = dot(probs.astype(jnp.bfloat16), grad)
            key_part = dot(terms, query)
            for s in range(2):
                rows = slice(s * BLK, (s + 1) * BLK)
                value_acc[unit * NBLK + u + s] = value_part[rows]
                key_acc[unit * NBLK + u + s] = key_part[rows]

    def step(turn, carry):
        for unit in range(2):
            for u in range(NBLK):
                row = unit * NBLK + u
                entry = list_ref[row, turn]
                bias = jnp.where(turn < count_ref[row], 0.0, FAR)
                query = q_ref[entry]
                grad = g_ref[entry]
                probs = jnp.exp2(dot(k_ref[unit, 0, u], query, NT) * SCALE2 - (lse_ref[entry] + bias))
                terms = (probs * (dot(v_ref[unit, 0, u], grad, NT) - d_ref[entry])).astype(jnp.bfloat16)
                value_acc[row] += dot(probs.astype(jnp.bfloat16), grad)
                key_acc[row] += dot(terms, query)
        return carry

    lax.fori_loop(0, trips_ref[0], step, 0)
    for unit in range(2):
        for u in range(NBLK):
            row = unit * NBLK + u
            dk_ref[unit, u] = (key_acc[row] * SCALE).astype(jnp.bfloat16)
            dv_ref[unit, u] = value_acc[row].astype(jnp.bfloat16)


def own_spec(rows, columns):
    return pl.BlockSpec((2, 1, NBLK, rows, columns), lambda g, member, *_: (0, member[0], 0, 0, 0))


def whole_spec(rows, columns):
    return pl.BlockSpec((2 * GROUP * NBLK, rows, columns), lambda *_: (0, 0, 0))


RESULT = pl.BlockSpec((2, NBLK, BLK, HEAD_DIM), lambda *_: (0, 0, 0, 0))
TOTALS = pl.BlockSpec((2, NBLK, 1, BLK), lambda *_: (0, 0, 0, 0))
PARAMS = pltpu.CompilerParams(vmem_limit_bytes=48 << 20)
LOW = jax.ShapeDtypeStruct((2, NBLK, BLK, HEAD_DIM), jnp.bfloat16)


def flat(array):
    return array.reshape((2 * GROUP * NBLK,) + array.shape[3:])


def query_pass(tables, query, grad, delta, key, value):
    return pl.pallas_call(
        query_kernel,
        out_shape=(LOW, jax.ShapeDtypeStruct((2, NBLK, 1, BLK), jnp.float32)),
        grid_spec=pltpu.PrefetchScalarGridSpec(
            num_scalar_prefetch=4,
            grid=(1,),
            in_specs=[
                own_spec(BLK, HEAD_DIM),
                own_spec(BLK, HEAD_DIM),
                own_spec(1, BLK),
                whole_spec(BLK, HEAD_DIM),
                whole_spec(BLK, HEAD_DIM),
            ],
            out_specs=(RESULT, TOTALS),
            scratch_shapes=[
                pltpu.VMEM((2 * NBLK, 1, BLK), jnp.float32),
                pltpu.VMEM((2 * NBLK, 1, BLK), jnp.float32),
                pltpu.VMEM((2 * NBLK, HEAD_DIM, BLK), jnp.float32),
            ],
        ),
        compiler_params=PARAMS,
        name="query_pass",
    )(*tables, query, grad, delta, flat(key), flat(value))


def key_pass(tables, key, value, delta, lse, query, grad):
    return pl.pallas_call(
        key_kernel,
        out_shape=(LOW, LOW),
        grid_spec=pltpu.PrefetchScalarGridSpec(
            num_scalar_prefetch=4,
            grid=(1,),
            in_specs=[
                own_spec(BLK, HEAD_DIM),
                own_spec(BLK, HEAD_DIM),
                whole_spec(1, BLK),
                whole_spec(1, BLK),
                whole_spec(BLK, HEAD_DIM),
                whole_spec(BLK, HEAD_DIM),
            ],
            out_specs=(RESULT, RESULT),
            scratch_shapes=[
                pltpu.VMEM((2 * NBLK, BLK, HEAD_DIM), jnp.float32),
                pltpu.VMEM((2 * NBLK, BLK, HEAD_DIM), jnp.float32),
            ],
        ),
        compiler_params=PARAMS,
        name="key_pass",
    )(*tables, key, value, flat(delta), flat(lse), flat(query), flat(grad))


def compact(live):
    rows = live.reshape(2 * NBLK, 2 * GROUP * NBLK)
    counts = jnp.sum(rows, axis=1)
    spot = jnp.arange(rows.shape[1], dtype=jnp.int32)
    ahead = jnp.sum(jnp.where(spot[None, :, None] > spot[None, None, :], rows[:, None, :], 0), axis=2)
    slot = jnp.arange(SLOTS, dtype=jnp.int32)
    match = (ahead[:, None, :] == slot[None, :, None]) & (rows[:, None, :] > 0)
    entries = jnp.sum(jnp.where(match, spot[None, None, :], 0), axis=2)
    return jnp.max(counts).reshape(1), counts, entries


def live_tables(frame_order, block_live, member):
    mine = jnp.stack([lax.dynamic_index_in_dim(frame_order, member, 0, False),
                      lax.dynamic_index_in_dim(frame_order, member + GROUP, 0, False)])
    distance = jnp.abs(mine[:, None] - frame_order[None, :])
    blocks = jnp.zeros((2, 2 * GROUP, NBLK, NBLK), jnp.int32)
    for d in range(1, 4):
        blocks = blocks + jnp.where((distance == d)[:, :, None, None], block_live[d][None, None], 0)
    return compact(blocks.transpose(0, 2, 1, 3)), compact(blocks.transpose(0, 3, 1, 2))


def local(queries, key_states, value_states, attn_out, grad_out, frame_order, block_live):
    _, half, member = place()
    products = grad_out.astype(jnp.float32) * attn_out.astype(jnp.float32)
    delta_local = jnp.sum(products.reshape(BLK, HEADS, HEAD_DIM), axis=2).T.reshape(HEADS, 1, BLK)
    where = member.astype(jnp.int32).reshape(1)
    by_query, by_key = live_tables(frame_order, block_live, member)
    key, value, query, grad, delta = gather_all(key_states, value_states, queries, grad_out, delta_local)
    dq, lse_own = query_pass((where, *by_query), query, grad, delta, key, value)
    lse = share_totals(lse_own)
    dk, dv = key_pass((where, *by_key), key, value, delta, lse, query, grad)
    swap = [(source, (source + GROUP) % (2 * GROUP)) for source in range(2 * GROUP)]

    def finish(result):
        result = result.reshape(2, NBLK * BLK, HEAD_DIM)
        kept = jnp.where(half == 0, result[0], result[1])
        sent = jnp.where(half == 0, result[1], result[0])
        came = lax.ppermute(sent, "frame", swap)
        return jnp.concatenate(
            [jnp.where(half == 0, kept, came), jnp.where(half == 0, came, kept)], axis=1
        )

    return finish(dq), finish(dk), finish(dv)


def solution(mesh):
    rows = P(("frame", "head"), None)
    out = P("frame", "head")
    return jax.shard_map(
        local,
        mesh=mesh,
        in_specs=(rows, rows, rows, rows, rows, P(), P()),
        out_specs=(out, out, out),
        check_vma=False,
    )
```

```python
import math

import jax
import jax.numpy as jnp
from jax import lax
from jax.experimental import pallas as pl
from jax.experimental.pallas import tpu as pltpu
from jax.sharding import PartitionSpec as P

HEADS = 16
HEAD_DIM = 128
SCALE = HEAD_DIM ** (-0.5)
SCALE2 = SCALE * math.log2(math.e)
REACH = 4
NBLK = 8
BLK = 128
RING = 4
GROUP = 8
ROWS = 2 * NBLK
ENTRIES = 2 * GROUP * NBLK
SLOTS = 2 * (REACH - 1) * NBLK
COUNT_AT = BLK - 1
CHUNK = 5
PAIR = 2
WIDE = 512
FAR = 1e30
MESH = pl.DeviceIdType.MESH
ANY = pl.BlockSpec(memory_space=pl.ANY)
SMEM = pl.BlockSpec(memory_space=pltpu.SMEM)
VMEM = pl.BlockSpec(memory_space=pltpu.VMEM)
NN = (((1,), (0,)), ((), ()))
NT = (((1,), (1,)), ((), ()))
TN = (((0,), (0,)), ((), ()))
KEY, VALUE, QUERY, GRAD, DELTA = range(5)


def dot(a, b, dims=NN):
    return lax.dot_general(a, b, dims, preferred_element_type=jnp.float32)


def place():
    frame = lax.axis_index("frame")
    return lax.axis_index("head"), frame // GROUP, frame % GROUP


class Ring:
    def __init__(self):
        self.head, self.half, self.member = place()
        ring, core = self.member // 2, self.member % 2
        up, down, far = (ring + 1) % RING, (ring + RING - 1) % RING, (ring + 2) % RING
        self.up, self.down, self.far = up * 2 + core, down * 2 + core, far * 2 + core
        self.twin = ring * 2 + 1 - core
        self.twin_up, self.twin_down, self.twin_far = up * 2 + 1 - core, down * 2 + 1 - core, far * 2 + 1 - core

    def device(self, slot):
        return {"head": self.head, "frame": self.half * GROUP + slot}


def remote(src, dst, send, recv, device):
    copy = pltpu.make_async_remote_copy(
        src_ref=src, dst_ref=dst, send_sem=send, recv_sem=recv, device_id=device, device_id_type=MESH
    )
    copy.start()
    return copy


def arrived(part, sem):
    pltpu.make_async_copy(part, part, sem).wait()


def live_list(flags):
    spot = lax.broadcasted_iota(jnp.int32, (ENTRIES, ENTRIES), 0)
    later = lax.broadcasted_iota(jnp.int32, (ENTRIES, ENTRIES), 1)
    before = jnp.where(spot < later, 1.0, 0.0).astype(jnp.bfloat16)
    ahead = dot(flags.astype(jnp.bfloat16), before)
    lane = lax.broadcasted_iota(jnp.int32, (ROWS, ENTRIES), 1)
    value = lane.astype(jnp.float32) * flags
    ahead = jnp.where(flags > 0.0, ahead, -1.0)
    table = jnp.where(lane == COUNT_AT, jnp.sum(flags, axis=1, keepdims=True), 0.0)
    for k in range(SLOTS):
        found = jnp.sum(jnp.where(ahead == float(k), value, 0.0), axis=1, keepdims=True)
        table = jnp.where(lane == k, found, table)
    return table.astype(jnp.int32)


def write_tables(member, order_ref, live_ref, by_query_ref, by_key_ref):
    lane = lax.broadcasted_iota(jnp.int32, (1, ENTRIES), 1)
    order = jnp.zeros((1, ENTRIES), jnp.int32)
    for g in range(2 * GROUP):
        order = jnp.where(lane // NBLK == g, order_ref[g], order)
    rows = lax.broadcasted_iota(jnp.int32, (NBLK, ENTRIES), 0)
    lanes = lax.broadcasted_iota(jnp.int32, (NBLK, ENTRIES), 1)
    spread = jnp.where(lanes % NBLK == rows, 1.0, 0.0).astype(jnp.bfloat16)
    query_rows, key_rows = [], []
    for unit in range(2):
        distance = jnp.abs(order - order_ref[unit * GROUP + member])
        by_query = jnp.zeros((NBLK, ENTRIES), jnp.float32)
        by_key = jnp.zeros((NBLK, ENTRIES), jnp.float32)
        for d in range(1, REACH):
            blocks = live_ref[d].astype(jnp.float32).astype(jnp.bfloat16)
            here = distance == d
            by_query = jnp.where(here, dot(blocks, spread), by_query)
            by_key = jnp.where(here, dot(blocks, spread, TN), by_key)
        query_rows.append(by_query)
        key_rows.append(by_key)
    by_query_ref[...] = live_list(jnp.concatenate(query_rows, axis=0))
    by_key_ref[...] = live_list(jnp.concatenate(key_rows, axis=0))


def gather_kernel(order_ref, live_ref, grad_ref, out_ref, key_src, value_src, query_src, grad_src, key_all, value_all,
                  query_all, grad_all, delta_all, query_own, grad_own, peak, total, acc, by_query_ref, by_key_ref,
                  delta_src, send1, recv1, send2, recv2, load):
    ring = Ring()
    head, half, member = ring.head, ring.half, ring.member
    plane = head * 2 + half
    srcs = (key_src, value_src, query_src, grad_src, delta_src)
    bufs = (key_all, value_all, query_all, grad_all, delta_all)

    def plane_peer(step):
        other = (plane + step) % HEADS
        return other, {"head": other // 2, "frame": (other % 2) * GROUP + member}

    barrier = pltpu.get_barrier_semaphore()
    for step in range(1, HEADS):
        pl.semaphore_signal(barrier, inc=1, device_id=plane_peer(step)[1], device_id_type=MESH)
    for slot in (ring.up, ring.down, ring.twin):
        pl.semaphore_signal(barrier, inc=1, device_id=ring.device(slot), device_id_type=MESH)
    pl.semaphore_wait(barrier, HEADS - 1 + 3)

    def column(a, other):
        if a == DELTA:
            return srcs[a].at[other]
        return srcs[a].at[:, pl.ds(pl.multiple_of(other * HEAD_DIM, HEAD_DIM), HEAD_DIM)]

    def scatter(a):
        target = bufs[a].at[half, member, head]
        for step in range(1, HEADS):
            other, device = plane_peer(step)
            remote(column(a, other), target, send1.at[a], recv1.at[a], device)
        pltpu.make_async_copy(column(a, plane), target, recv1.at[a]).start()

    for a in (KEY, VALUE, QUERY, GRAD):
        scatter(a)
    for n in range(HEADS):
        lanes = slice(n * HEAD_DIM, (n + 1) * HEAD_DIM)
        products = grad_ref[:, lanes].astype(jnp.float32) * out_ref[:, lanes].astype(jnp.float32)
        delta_src[n] = jnp.sum(products.T, axis=0, keepdims=True)
    scatter(DELTA)

    pending = []

    def push(a, number, part, slot, arrive):
        pending.append(remote(part, part, send2.at[a, number], recv2.at[a, arrive], ring.device(slot)))

    for a in (KEY, VALUE, QUERY, GRAD, DELTA):
        own = bufs[a].at[:, member]
        arrived(own, recv1.at[a])
        push(a, 0, own, ring.up, 0)
        push(a, 1, own, ring.down, 1)
        push(a, 2, own, ring.twin, 4)
        if a in (QUERY, GRAD):
            kept = query_own if a == QUERY else grad_own
            pltpu.make_async_copy(own, kept, load.at[a - QUERY]).start()
        if a == KEY:
            write_tables(member, order_ref, live_ref, by_query_ref, by_key_ref)
    pltpu.make_async_copy(bufs[QUERY].at[:, member], query_own, load.at[0]).wait()
    pltpu.make_async_copy(bufs[GRAD].at[:, member], grad_own, load.at[1]).wait()

    span = WIDE // BLK
    for unit in range(2):
        key = key_all[unit, member].reshape(NBLK * BLK, HEAD_DIM)
        value = value_all[unit, member].reshape(NBLK * BLK, HEAD_DIM)
        for i in range(0, NBLK, span):
            query = query_own[unit, i : i + span].reshape(WIDE, HEAD_DIM)
            grad = grad_own[unit, i : i + span].reshape(WIDE, HEAD_DIM)
            delta = jnp.concatenate([delta_all[unit, member, i + s] for s in range(span)], axis=1)
            scores = dot(key, query, NT) * SCALE2
            top = jnp.max(scores, axis=0, keepdims=True)
            probs = jnp.exp2(scores - top)
            summed = jnp.sum(probs, axis=0, keepdims=True)
            terms = (probs * (dot(value, grad, NT) - delta)).astype(jnp.bfloat16)
            partial = dot(key, terms, TN)
            for s in range(span):
                lanes = slice(s * BLK, (s + 1) * BLK)
                row = unit * NBLK + i + s
                peak[row] = top[:, lanes]
                total[row] = summed[:, lanes]
                acc[row] = partial[:, lanes]

    for a in (KEY, VALUE, QUERY, GRAD, DELTA):
        part = bufs[a].at[:, ring.down]
        arrived(part, recv2.at[a, 0])
        if a not in (QUERY, GRAD):
            push(a, 3, bufs[a].at[0, ring.down], ring.up, 2)
        push(a, 4, part, ring.twin, 5)
        part = bufs[a].at[:, ring.up]
        arrived(part, recv2.at[a, 1])
        if a not in (QUERY, GRAD):
            push(a, 5, bufs[a].at[1, ring.up], ring.down, 3)
        push(a, 6, part, ring.twin, 6)
    for a in (KEY, VALUE, DELTA):
        part = bufs[a].at[0, ring.far]
        arrived(part, recv2.at[a, 2])
        push(a, 7, part, ring.twin, 7)
        part = bufs[a].at[1, ring.far]
        arrived(part, recv2.at[a, 3])
        push(a, 8, part, ring.twin, 8)
    for a in (KEY, VALUE, QUERY, GRAD, DELTA):
        arrived(bufs[a].at[:, ring.twin], recv2.at[a, 4])
        arrived(bufs[a].at[:, ring.twin_down], recv2.at[a, 5])
        arrived(bufs[a].at[:, ring.twin_up], recv2.at[a, 6])
        if a not in (QUERY, GRAD):
            arrived(bufs[a].at[0, ring.twin_far], recv2.at[a, 7])
            arrived(bufs[a].at[1, ring.twin_far], recv2.at[a, 8])
    for copy in pending:
        copy.wait_send()
    for a in range(5):
        sent = srcs[a].at[pl.ds(0, HEADS - 1)] if a == DELTA else srcs[a].at[:, pl.ds(0, (HEADS - 1) * HEAD_DIM)]
        arrived(sent, send1.at[a])


WHOLE = (2, GROUP, NBLK, BLK, HEAD_DIM)
STATS = (2, GROUP, NBLK, 1, BLK)
OWN = (2, NBLK, BLK, HEAD_DIM)
LIMIT = 24 << 20


def gather_all(order, live, key, value, query, grad, out):
    low, full, whole = jnp.bfloat16, jnp.float32, jnp.int32
    return pl.pallas_call(
        gather_kernel,
        out_shape=(
            jax.ShapeDtypeStruct(WHOLE, low),
            jax.ShapeDtypeStruct(WHOLE, low),
            jax.ShapeDtypeStruct(WHOLE, low),
            jax.ShapeDtypeStruct(WHOLE, low),
            jax.ShapeDtypeStruct(STATS, full),
            jax.ShapeDtypeStruct(OWN, low),
            jax.ShapeDtypeStruct(OWN, low),
            jax.ShapeDtypeStruct((ROWS, 1, BLK), full),
            jax.ShapeDtypeStruct((ROWS, 1, BLK), full),
            jax.ShapeDtypeStruct((ROWS, HEAD_DIM, BLK), full),
            jax.ShapeDtypeStruct((ROWS, ENTRIES), whole),
            jax.ShapeDtypeStruct((ROWS, ENTRIES), whole),
        ),
        in_specs=[SMEM, VMEM, VMEM, VMEM, ANY, ANY, ANY, ANY],
        out_specs=(VMEM, VMEM, ANY, ANY) + (VMEM,) * 8,
        scratch_shapes=[
            pltpu.VMEM((HEADS, 1, BLK), full),
            pltpu.SemaphoreType.DMA((5,)),
            pltpu.SemaphoreType.DMA((5,)),
            pltpu.SemaphoreType.DMA((5, 9)),
            pltpu.SemaphoreType.DMA((5, 9)),
            pltpu.SemaphoreType.DMA((2,)),
        ],
        compiler_params=pltpu.CompilerParams(collective_id=0, has_side_effects=True, vmem_limit_bytes=LIMIT),
        name="gather_all",
    )(order, live, grad, out, key, value, query, grad)


def turns(table, rows):
    most = table[rows[0], COUNT_AT]
    for row in rows[1:]:
        most = jnp.maximum(most, table[row, COUNT_AT])
    return (most + CHUNK - 1) // CHUNK


def query_kernel(table, query_own, grad_own, delta_all, key_ref, value_ref, peak_in, total_in, acc_in, dq_ref, lse_ref,
                 peak, total, acc):
    member = place()[2]
    peak[...] = peak_in[...]
    total[...] = total_in[...]
    acc[...] = acc_in[...]

    def step(turn, carry):
        for first in range(0, ROWS, PAIR):
            rows = range(first, first + PAIR)
            keys, scores, grads = [], [], []
            for row in rows:
                unit, i = row // NBLK, row % NBLK
                slots = [turn * CHUNK + c for c in range(CHUNK)]
                entries = [table[row, slot] for slot in slots]
                bias = [jnp.where(slot < table[row, COUNT_AT], 0.0, -FAR) for slot in slots]
                key = jnp.concatenate([key_ref[e] for e in entries], axis=0)
                value = jnp.concatenate([value_ref[e] for e in entries], axis=0)
                s = dot(key, query_own[unit, i], NT)
                s = jnp.concatenate([s[c * BLK : (c + 1) * BLK] * SCALE2 + bias[c] for c in range(CHUNK)], axis=0)
                keys.append(key)
                scores.append(s)
                grads.append(dot(value, grad_own[unit, i], NT) - delta_all[unit, member, i])
            results = []
            for n, row in enumerate(rows):
                before = peak[row]
                top = jnp.maximum(before, jnp.max(scores[n], axis=0, keepdims=True))
                probs = jnp.exp2(scores[n] - top)
                terms = (probs * grads[n]).astype(jnp.bfloat16)
                results.append((top, jnp.exp2(before - top), jnp.sum(probs, axis=0, keepdims=True), dot(keys[n], terms, TN)))
            for n, row in enumerate(rows):
                top, shrink, summed, product = results[n]
                peak[row] = top
                total[row] = total[row] * shrink + summed
                acc[row] = acc[row] * shrink + product
        return carry

    lax.fori_loop(0, turns(table, range(ROWS)), step, 0)
    for row in range(ROWS):
        unit, i = row // NBLK, row % NBLK
        lse_ref[unit, i] = peak[row] + jnp.log2(total[row])
        dq_ref[unit, i] = (acc[row] * (SCALE / total[row])).T.astype(jnp.bfloat16)


def flat(array):
    return array.reshape((ENTRIES,) + array.shape[3:])


def query_pass(table, query_own, grad_own, delta, key, value, peak, total, acc):
    return pl.pallas_call(
        query_kernel,
        out_shape=(jax.ShapeDtypeStruct(OWN, jnp.bfloat16), jax.ShapeDtypeStruct((2, NBLK, 1, BLK), jnp.float32)),
        in_specs=[SMEM] + [VMEM] * 8,
        out_specs=(VMEM, VMEM),
        scratch_shapes=[
            pltpu.VMEM((ROWS, 1, BLK), jnp.float32),
            pltpu.VMEM((ROWS, 1, BLK), jnp.float32),
            pltpu.VMEM((ROWS, HEAD_DIM, BLK), jnp.float32),
        ],
        compiler_params=pltpu.CompilerParams(vmem_limit_bytes=LIMIT),
        name="query_pass",
    )(table, query_own, grad_own, delta, flat(key), flat(value), peak, total, acc)


def share_kernel(lse_own, delta_all, query_own, grad_own, key_all, value_all, query_part, grad_part, lse_all, query_all,
                 grad_all, key_acc, value_acc, send, recv, send2, recv2, load):
    ring = Ring()
    member = ring.member

    barrier = pltpu.get_barrier_semaphore()
    for step in range(1, GROUP):
        slot = (member + step) % GROUP
        pl.semaphore_signal(barrier, inc=1, device_id=ring.device(slot), device_id_type=MESH)
    pl.semaphore_wait(barrier, GROUP - 1)
    pending = []
    for step in range(1, GROUP):
        device = ring.device((member + step) % GROUP)
        pending.append(remote(lse_own, lse_all.at[:, member], send.at[step], recv.at[step], device))
    mine = pltpu.make_async_copy(lse_own, lse_all.at[:, member], load.at[2, 0])
    mine.start()
    parts, alls = (query_part, grad_part), (query_all, grad_all)
    for a in range(2):
        pending.append(
            remote(parts[a].at[0, ring.down], alls[a].at[0, ring.down], send2.at[a, 0], recv2.at[a, 0], ring.device(ring.up))
        )
        pending.append(
            remote(parts[a].at[1, ring.up], alls[a].at[1, ring.up], send2.at[a, 1], recv2.at[a, 1], ring.device(ring.down))
        )
    held = (ring.member, ring.up, ring.down, ring.twin, ring.twin_up, ring.twin_down)
    loads = []
    for a in range(2):
        for n, slot in enumerate(held):
            loads.append(pltpu.make_async_copy(parts[a].at[:, slot], alls[a].at[:, slot], load.at[a, n]))
            loads[-1].start()

    def relay(n):
        for a in range(2):
            part = alls[a].at[n, ring.far]
            arrived(part, recv2.at[a, n])
            pending.append(remote(part, part, send2.at[a, 2 + n], recv2.at[a, 2 + n], ring.device(ring.twin)))

    for unit in range(2):
        query = query_own[unit].reshape(NBLK * BLK, HEAD_DIM)
        grad = grad_own[unit].reshape(NBLK * BLK, HEAD_DIM)
        delta = jnp.concatenate([delta_all[unit, member, i] for i in range(NBLK)], axis=1)
        lse = jnp.concatenate([lse_own[unit, i] for i in range(NBLK)], axis=1)
        span = WIDE // BLK
        for u in range(0, NBLK, span):
            key = key_all[unit, member, u : u + span].reshape(WIDE, HEAD_DIM)
            value = value_all[unit, member, u : u + span].reshape(WIDE, HEAD_DIM)
            probs = jnp.exp2(dot(key, query, NT) * SCALE2 - lse)
            terms = (probs * (dot(value, grad, NT) - delta)).astype(jnp.bfloat16)
            value_part = dot(probs.astype(jnp.bfloat16), grad)
            key_part = dot(terms, query)
            for s in range(span):
                rows = slice(s * BLK, (s + 1) * BLK)
                value_acc[unit * NBLK + u + s] = value_part[rows]
                key_acc[unit * NBLK + u + s] = key_part[rows]

    relay(0)
    relay(1)
    mine.wait()
    for copy in loads:
        copy.wait()
    for step in range(1, GROUP):
        arrived(lse_own, recv.at[step])
    for a in range(2):
        arrived(alls[a].at[0, ring.twin_far], recv2.at[a, 2])
        arrived(alls[a].at[1, ring.twin_far], recv2.at[a, 3])
    for copy in pending:
        copy.wait_send()


def share_totals(lse_own, delta, query_own, grad_own, key, value, query, grad):
    return pl.pallas_call(
        share_kernel,
        out_shape=(
            jax.ShapeDtypeStruct(STATS, jnp.float32),
            jax.ShapeDtypeStruct(WHOLE, jnp.bfloat16),
            jax.ShapeDtypeStruct(WHOLE, jnp.bfloat16),
            jax.ShapeDtypeStruct((ROWS, BLK, HEAD_DIM), jnp.float32),
            jax.ShapeDtypeStruct((ROWS, BLK, HEAD_DIM), jnp.float32),
        ),
        in_specs=[VMEM] * 6 + [ANY] * 2,
        out_specs=(VMEM,) * 5,
        scratch_shapes=[
            pltpu.SemaphoreType.DMA((GROUP,)),
            pltpu.SemaphoreType.DMA((GROUP,)),
            pltpu.SemaphoreType.DMA((2, 4)),
            pltpu.SemaphoreType.DMA((2, 4)),
            pltpu.SemaphoreType.DMA((3, 6)),
        ],
        compiler_params=pltpu.CompilerParams(collective_id=1, has_side_effects=True, vmem_limit_bytes=LIMIT),
        name="share_totals",
    )(lse_own, delta, query_own, grad_own, key, value, query, grad)


def key_kernel(other, table, key_all, value_all, delta_ref, lse_ref, query_ref, grad_ref, key_in, value_in, out_ref,
               key_acc, value_acc):
    _, half, member = place()
    unit = 1 - half if other else half
    base = unit * NBLK
    for u in range(NBLK):
        key_acc[u] = key_in[base + u]
        value_acc[u] = value_in[base + u]

    def step(turn, carry):
        for first in range(0, NBLK, PAIR):
            blocks = range(first, first + PAIR)
            loads, results = [], []
            for u in blocks:
                row = base + u
                slots = [turn * CHUNK + c for c in range(CHUNK)]
                entries = [table[row, slot] for slot in slots]
                bias = [jnp.where(slot < table[row, COUNT_AT], 0.0, FAR) for slot in slots]
                query = jnp.concatenate([query_ref[e] for e in entries], axis=0)
                grad = jnp.concatenate([grad_ref[e] for e in entries], axis=0)
                lse = jnp.concatenate([lse_ref[e] + b for e, b in zip(entries, bias)], axis=1)
                delta = jnp.concatenate([delta_ref[e] for e in entries], axis=1)
                scores = dot(key_all[unit, member, u], query, NT)
                grads = dot(value_all[unit, member, u], grad, NT)
                loads.append((query, grad, lse, delta, scores, grads))
            for query, grad, lse, delta, scores, grads in loads:
                probs = jnp.exp2(scores * SCALE2 - lse)
                terms = (probs * (grads - delta)).astype(jnp.bfloat16)
                results.append((dot(probs.astype(jnp.bfloat16), grad), dot(terms, query)))
            for n, u in enumerate(blocks):
                value_acc[u] += results[n][0]
                key_acc[u] += results[n][1]
        return carry

    lax.fori_loop(0, turns(table, [base + u for u in range(NBLK)]), step, 0)
    for u in range(NBLK):
        out_ref[0, u] = (key_acc[u] * SCALE).astype(jnp.bfloat16)
        out_ref[1, u] = value_acc[u].astype(jnp.bfloat16)


def key_pass(other, table, key, value, delta, lse, query, grad, key_acc, value_acc):
    def kernel(*refs):
        key_kernel(other, *refs)

    return pl.pallas_call(
        kernel,
        out_shape=jax.ShapeDtypeStruct(OWN, jnp.bfloat16),
        in_specs=[SMEM] + [VMEM] * 8,
        out_specs=VMEM,
        scratch_shapes=[
            pltpu.VMEM((NBLK, BLK, HEAD_DIM), jnp.float32),
            pltpu.VMEM((NBLK, BLK, HEAD_DIM), jnp.float32),
        ],
        compiler_params=pltpu.CompilerParams(vmem_limit_bytes=LIMIT),
        cost_estimate=pl.CostEstimate(flops=2_000_000_000, bytes_accessed=1 << 20, transcendentals=1 << 20),
        name="key_pass_sent" if other else "key_pass_kept",
    )(table, key, value, flat(delta), flat(lse), flat(query), flat(grad), key_acc, value_acc)


def local(queries, key_states, value_states, attn_out, grad_out, frame_order, block_live):
    half = place()[1]
    (key, value, query, grad, delta, query_own, grad_own, peak, total, acc, by_query, by_key) = gather_all(
        frame_order, block_live, key_states, value_states, queries, grad_out, attn_out
    )
    dq, lse_own = query_pass(by_query, query_own, grad_own, delta, key, value, peak, total, acc)
    swap = [(source, (source + GROUP) % (2 * GROUP)) for source in range(2 * GROUP)]

    def across(sent):
        return lax.ppermute(sent, "frame", swap)

    def join(kept, came):
        kept, came = kept.reshape(NBLK * BLK, HEAD_DIM), came.reshape(NBLK * BLK, HEAD_DIM)
        return jnp.concatenate([jnp.where(half == 0, kept, came), jnp.where(half == 0, came, kept)], axis=1)

    dq_came = across(jnp.where(half == 0, dq[1], dq[0]))
    lse, query, grad, key_acc, value_acc = share_totals(lse_own, delta, query_own, grad_own, key, value, query, grad)
    sums = (by_key, key, value, delta, lse, query, grad, key_acc, value_acc)
    came = across(key_pass(True, *sums))
    kept = key_pass(False, *sums)
    return join(jnp.where(half == 0, dq[0], dq[1]), dq_came), join(kept[0], came[0]), join(kept[1], came[1])


def solution(mesh):
    rows = P(("frame", "head"), None)
    out = P("frame", "head")
    return jax.shard_map(
        local,
        mesh=mesh,
        in_specs=(rows, rows, rows, rows, rows, P(), P()),
        out_specs=(out, out, out),
        check_vma=False,
    )
```

```python
import math

import jax
import jax.numpy as jnp
from jax import lax
from jax.experimental import pallas as pl
from jax.experimental.pallas import tpu as pltpu
from jax.sharding import PartitionSpec as P

HEADS = 16
HEAD_DIM = 128
SCALE = HEAD_DIM ** (-0.5)
SCALE2 = SCALE * math.log2(math.e)
REACH = 4
NBLK = 8
BLK = 128
RING = 4
GROUP = 8
ROWS = 2 * NBLK
ENTRIES = 2 * GROUP * NBLK
SLOTS = 2 * (REACH - 1) * NBLK
COUNT_AT = BLK - 1
CHUNK = 5
PAIR = 2
WIDE = 512
FAR = 1e30
MESH = pl.DeviceIdType.MESH
ANY = pl.BlockSpec(memory_space=pl.ANY)
SMEM = pl.BlockSpec(memory_space=pltpu.SMEM)
HBM = pl.BlockSpec(memory_space=pltpu.HBM)
VMEM = pl.BlockSpec(memory_space=pltpu.VMEM)
NN = (((1,), (0,)), ((), ()))
NT = (((1,), (1,)), ((), ()))
TN = (((0,), (0,)), ((), ()))
KEY, VALUE, QUERY, GRAD, DELTA = range(5)


def dot(a, b, dims=NN):
    return lax.dot_general(a, b, dims, preferred_element_type=jnp.float32)


def place():
    frame = lax.axis_index("frame")
    return lax.axis_index("head"), frame // GROUP, frame % GROUP


class Ring:
    def __init__(self):
        self.head, self.half, self.member = place()
        ring, core = self.member // 2, self.member % 2
        up, down, far = (ring + 1) % RING, (ring + RING - 1) % RING, (ring + 2) % RING
        self.up, self.down, self.far = up * 2 + core, down * 2 + core, far * 2 + core
        self.twin = ring * 2 + 1 - core
        self.twin_up, self.twin_down, self.twin_far = up * 2 + 1 - core, down * 2 + 1 - core, far * 2 + 1 - core

    def device(self, slot):
        return {"head": self.head, "frame": self.half * GROUP + slot}


def remote(src, dst, send, recv, device):
    copy = pltpu.make_async_remote_copy(
        src_ref=src, dst_ref=dst, send_sem=send, recv_sem=recv, device_id=device, device_id_type=MESH
    )
    copy.start()
    return copy


def arrived(part, sem):
    pltpu.make_async_copy(part, part, sem).wait()


def live_list(flags):
    spot = lax.broadcasted_iota(jnp.int32, (ENTRIES, ENTRIES), 0)
    later = lax.broadcasted_iota(jnp.int32, (ENTRIES, ENTRIES), 1)
    before = jnp.where(spot < later, 1.0, 0.0).astype(jnp.bfloat16)
    ahead = dot(flags.astype(jnp.bfloat16), before)
    lane = lax.broadcasted_iota(jnp.int32, (ROWS, ENTRIES), 1)
    value = lane.astype(jnp.float32) * flags
    ahead = jnp.where(flags > 0.0, ahead, -1.0)
    table = jnp.where(lane == COUNT_AT, jnp.sum(flags, axis=1, keepdims=True), 0.0)
    for k in range(SLOTS):
        found = jnp.sum(jnp.where(ahead == float(k), value, 0.0), axis=1, keepdims=True)
        table = jnp.where(lane == k, found, table)
    return table.astype(jnp.int32)


def write_tables(member, order_ref, live_ref, by_query_ref, by_key_ref):
    lane = lax.broadcasted_iota(jnp.int32, (1, ENTRIES), 1)
    order = jnp.zeros((1, ENTRIES), jnp.int32)
    for g in range(2 * GROUP):
        order = jnp.where(lane // NBLK == g, order_ref[g], order)
    rows = lax.broadcasted_iota(jnp.int32, (NBLK, ENTRIES), 0)
    lanes = lax.broadcasted_iota(jnp.int32, (NBLK, ENTRIES), 1)
    spread = jnp.where(lanes % NBLK == rows, 1.0, 0.0).astype(jnp.bfloat16)
    query_rows, key_rows = [], []
    for unit in range(2):
        distance = jnp.abs(order - order_ref[unit * GROUP + member])
        by_query = jnp.zeros((NBLK, ENTRIES), jnp.float32)
        by_key = jnp.zeros((NBLK, ENTRIES), jnp.float32)
        for d in range(1, REACH):
            blocks = live_ref[d].astype(jnp.float32).astype(jnp.bfloat16)
            here = distance == d
            by_query = jnp.where(here, dot(blocks, spread), by_query)
            by_key = jnp.where(here, dot(blocks, spread, TN), by_key)
        query_rows.append(by_query)
        key_rows.append(by_key)
    by_query_ref[...] = live_list(jnp.concatenate(query_rows, axis=0))
    by_key_ref[...] = live_list(jnp.concatenate(key_rows, axis=0))


def gather_kernel(order_src, live_src, out_src, key_src, value_src, query_src, grad_src, key_all, value_all, query_all,
                  grad_all, delta_all, query_own, grad_own, peak, total, acc, by_query_ref, by_key_ref, delta_src, raw,
                  grad_raw, out_raw, order_ref, live_ref, send1, recv1, send2, recv2, send3, recv3, load):
    ring = Ring()
    head, half, member = ring.head, ring.half, ring.member
    plane = head * 2 + half
    srcs = (key_src, value_src, query_src, grad_src, delta_src)
    bufs = (key_all, value_all, query_all, grad_all, delta_all)

    def plane_peer(step):
        other = (plane + step) % HEADS
        return other, {"head": other // 2, "frame": (other % 2) * GROUP + member}

    fetches = [
        pltpu.make_async_copy(grad_src, grad_raw, load.at[0]),
        pltpu.make_async_copy(out_src, out_raw, load.at[1]),
        pltpu.make_async_copy(order_src, order_ref, load.at[2]),
        pltpu.make_async_copy(live_src, live_ref, load.at[3]),
    ]
    for fetch in fetches:
        fetch.start()
    barrier = pltpu.get_barrier_semaphore()
    for step in range(1, HEADS):
        pl.semaphore_signal(barrier, inc=1, device_id=plane_peer(step)[1], device_id_type=MESH)
    for slot in (ring.up, ring.down, ring.twin):
        pl.semaphore_signal(barrier, inc=1, device_id=ring.device(slot), device_id_type=MESH)
    pl.semaphore_wait(barrier, HEADS - 1 + 3)

    pending = []
    pending.append(remote(query_src, raw.at[0], send3.at[0], recv3.at[0], ring.device(ring.up)))
    pending.append(remote(query_src, raw.at[1], send3.at[1], recv3.at[1], ring.device(ring.down)))

    def column(src, other):
        if src is delta_src:
            return src.at[other]
        return src.at[:, pl.ds(pl.multiple_of(other * HEAD_DIM, HEAD_DIM), HEAD_DIM)]

    def scatter(src, target, send, recv):
        for step in range(1, HEADS):
            other, device = plane_peer(step)
            remote(column(src, other), target, send, recv, device)
        pltpu.make_async_copy(column(src, plane), target, recv).start()

    for a in (KEY, VALUE, QUERY, GRAD):
        scatter(srcs[a], bufs[a].at[half, member, head], send1.at[a], recv1.at[a])
    fetches[0].wait()
    fetches[1].wait()
    for n in range(HEADS):
        lanes = slice(n * HEAD_DIM, (n + 1) * HEAD_DIM)
        products = grad_raw[:, lanes].astype(jnp.float32) * out_raw[:, lanes].astype(jnp.float32)
        delta_src[n] = jnp.sum(products.T, axis=0, keepdims=True)
    scatter(delta_src, bufs[DELTA].at[half, member, head], send1.at[DELTA], recv1.at[DELTA])

    def push(a, number, part, slot, arrive):
        pending.append(remote(part, part, send2.at[a, number], recv2.at[a, arrive], ring.device(slot)))

    def spread(a):
        own = bufs[a].at[:, member]
        arrived(own, recv1.at[a])
        if a != QUERY:
            push(a, 0, own, ring.up, 0)
            push(a, 1, own, ring.down, 1)
        push(a, 2, own, ring.twin, 4)

    def pass_raw(number, slot):
        scatter(raw.at[number], bufs[QUERY].at[half, slot, head], send1.at[5 + number], recv1.at[5 + number])

    upper, lower = pl.ds(0, BLK // 2), pl.ds(BLK // 2, BLK // 2)
    spread(KEY)
    fetches[2].wait()
    fetches[3].wait()
    write_tables(member, order_ref, live_ref, by_query_ref, by_key_ref)
    spread(VALUE)
    arrived(raw.at[0], recv3.at[0])
    pending.append(remote(raw.at[0, upper], raw.at[2, upper], send3.at[2], recv3.at[2], ring.device(ring.up)))
    pass_raw(0, ring.down)
    arrived(raw.at[1], recv3.at[1])
    pending.append(remote(raw.at[1, lower], raw.at[2, lower], send3.at[3], recv3.at[3], ring.device(ring.down)))
    pass_raw(1, ring.up)
    spread(QUERY)
    fetch_query = pltpu.make_async_copy(bufs[QUERY].at[:, member], query_own, load.at[4])
    fetch_query.start()
    spread(GRAD)
    fetch_grad = pltpu.make_async_copy(bufs[GRAD].at[:, member], grad_own, load.at[5])
    fetch_grad.start()
    spread(DELTA)
    fetch_query.wait()
    fetch_grad.wait()

    span = WIDE // BLK
    for unit in range(2):
        key = key_all[unit, member].reshape(NBLK * BLK, HEAD_DIM)
        value = value_all[unit, member].reshape(NBLK * BLK, HEAD_DIM)
        for i in range(0, NBLK, span):
            query = query_own[unit, i : i + span].reshape(WIDE, HEAD_DIM)
            grad = grad_own[unit, i : i + span].reshape(WIDE, HEAD_DIM)
            delta = jnp.concatenate([delta_all[unit, member, i + s] for s in range(span)], axis=1)
            scores = dot(key, query, NT) * SCALE2
            top = jnp.max(scores, axis=0, keepdims=True)
            probs = jnp.exp2(scores - top)
            summed = jnp.sum(probs, axis=0, keepdims=True)
            terms = (probs * (dot(value, grad, NT) - delta)).astype(jnp.bfloat16)
            partial = dot(key, terms, TN)
            for s in range(span):
                lanes = slice(s * BLK, (s + 1) * BLK)
                row = unit * NBLK + i + s
                peak[row] = top[:, lanes]
                total[row] = summed[:, lanes]
                acc[row] = partial[:, lanes]

    arrived(raw.at[2, upper], recv3.at[2])
    arrived(raw.at[2, lower], recv3.at[3])
    pass_raw(2, ring.far)
    arrived(bufs[QUERY].at[:, ring.down], recv1.at[5])
    push(QUERY, 4, bufs[QUERY].at[:, ring.down], ring.twin, 5)
    arrived(bufs[QUERY].at[:, ring.up], recv1.at[6])
    push(QUERY, 6, bufs[QUERY].at[:, ring.up], ring.twin, 6)
    for a in (KEY, VALUE, GRAD, DELTA):
        part = bufs[a].at[:, ring.down]
        arrived(part, recv2.at[a, 0])
        if a != GRAD:
            push(a, 3, bufs[a].at[0, ring.down], ring.up, 2)
        push(a, 4, part, ring.twin, 5)
        part = bufs[a].at[:, ring.up]
        arrived(part, recv2.at[a, 1])
        if a != GRAD:
            push(a, 5, bufs[a].at[1, ring.up], ring.down, 3)
        push(a, 6, part, ring.twin, 6)
    arrived(bufs[QUERY].at[:, ring.far], recv1.at[7])
    push(QUERY, 7, bufs[QUERY].at[:, ring.far], ring.twin, 7)
    for a in (KEY, VALUE, DELTA):
        part = bufs[a].at[0, ring.far]
        arrived(part, recv2.at[a, 2])
        push(a, 7, part, ring.twin, 7)
        part = bufs[a].at[1, ring.far]
        arrived(part, recv2.at[a, 3])
        push(a, 8, part, ring.twin, 8)
    for a in (KEY, VALUE, QUERY, GRAD, DELTA):
        arrived(bufs[a].at[:, ring.twin], recv2.at[a, 4])
        arrived(bufs[a].at[:, ring.twin_down], recv2.at[a, 5])
        arrived(bufs[a].at[:, ring.twin_up], recv2.at[a, 6])
        if a == QUERY:
            arrived(bufs[a].at[:, ring.twin_far], recv2.at[a, 7])
        elif a != GRAD:
            arrived(bufs[a].at[0, ring.twin_far], recv2.at[a, 7])
            arrived(bufs[a].at[1, ring.twin_far], recv2.at[a, 8])
    for copy in pending:
        copy.wait_send()
    for a in range(8):
        source = srcs[a] if a < 5 else raw.at[a - 5]
        sent = source.at[pl.ds(0, HEADS - 1)] if a == DELTA else source.at[:, pl.ds(0, (HEADS - 1) * HEAD_DIM)]
        arrived(sent, send1.at[a])


WHOLE = (2, GROUP, NBLK, BLK, HEAD_DIM)
STATS = (2, GROUP, NBLK, 1, BLK)
OWN = (2, NBLK, BLK, HEAD_DIM)
LIMIT = 24 << 20


def gather_all(order, live, key, value, query, grad, out):
    low, full, whole = jnp.bfloat16, jnp.float32, jnp.int32
    return pl.pallas_call(
        gather_kernel,
        out_shape=(
            jax.ShapeDtypeStruct(WHOLE, low),
            jax.ShapeDtypeStruct(WHOLE, low),
            jax.ShapeDtypeStruct(WHOLE, low),
            jax.ShapeDtypeStruct(WHOLE, low),
            jax.ShapeDtypeStruct(STATS, full),
            jax.ShapeDtypeStruct(OWN, low),
            jax.ShapeDtypeStruct(OWN, low),
            jax.ShapeDtypeStruct((ROWS, 1, BLK), full),
            jax.ShapeDtypeStruct((ROWS, 1, BLK), full),
            jax.ShapeDtypeStruct((ROWS, HEAD_DIM, BLK), full),
            jax.ShapeDtypeStruct((ROWS, ENTRIES), whole),
            jax.ShapeDtypeStruct((ROWS, ENTRIES), whole),
        ),
        in_specs=[HBM] * 7,
        out_specs=(VMEM, VMEM, VMEM, ANY) + (VMEM,) * 8,
        scratch_shapes=[
            pltpu.VMEM((HEADS, 1, BLK), full),
            pltpu.VMEM((3, BLK, HEADS * HEAD_DIM), low),
            pltpu.VMEM((BLK, HEADS * HEAD_DIM), low),
            pltpu.VMEM((BLK, HEADS * HEAD_DIM), low),
            pltpu.SMEM((2 * GROUP,), whole),
            pltpu.VMEM((2 * GROUP, NBLK, NBLK), whole),
            pltpu.SemaphoreType.DMA((8,)),
            pltpu.SemaphoreType.DMA((8,)),
            pltpu.SemaphoreType.DMA((5, 9)),
            pltpu.SemaphoreType.DMA((5, 9)),
            pltpu.SemaphoreType.DMA((4,)),
            pltpu.SemaphoreType.DMA((4,)),
            pltpu.SemaphoreType.DMA((6,)),
        ],
        compiler_params=pltpu.CompilerParams(collective_id=0, has_side_effects=True, vmem_limit_bytes=LIMIT),
        name="gather_all",
    )(order, live, out, key, value, query, grad)


def turns(table, rows):
    most = table[rows[0], COUNT_AT]
    for row in rows[1:]:
        most = jnp.maximum(most, table[row, COUNT_AT])
    return (most + CHUNK - 1) // CHUNK


def query_kernel(table, query_own, grad_own, delta_all, key_ref, value_ref, peak_in, total_in, acc_in, dq_ref, lse_ref,
                 peak, total, acc):
    member = place()[2]
    peak[...] = peak_in[...]
    total[...] = total_in[...]
    acc[...] = acc_in[...]

    def step(turn, carry):
        for first in range(0, ROWS, PAIR):
            rows = range(first, first + PAIR)
            keys, scores, grads = [], [], []
            for row in rows:
                unit, i = row // NBLK, row % NBLK
                slots = [turn * CHUNK + c for c in range(CHUNK)]
                entries = [table[row, slot] for slot in slots]
                bias = [jnp.where(slot < table[row, COUNT_AT], 0.0, -FAR) for slot in slots]
                key = jnp.concatenate([key_ref[e] for e in entries], axis=0)
                value = jnp.concatenate([value_ref[e] for e in entries], axis=0)
                s = dot(key, query_own[unit, i], NT)
                s = jnp.concatenate([s[c * BLK : (c + 1) * BLK] * SCALE2 + bias[c] for c in range(CHUNK)], axis=0)
                keys.append(key)
                scores.append(s)
                grads.append(dot(value, grad_own[unit, i], NT) - delta_all[unit, member, i])
            results = []
            for n, row in enumerate(rows):
                before = peak[row]
                top = jnp.maximum(before, jnp.max(scores[n], axis=0, keepdims=True))
                probs = jnp.exp2(scores[n] - top)
                terms = (probs * grads[n]).astype(jnp.bfloat16)
                results.append((top, jnp.exp2(before - top), jnp.sum(probs, axis=0, keepdims=True), dot(keys[n], terms, TN)))
            for n, row in enumerate(rows):
                top, shrink, summed, product = results[n]
                peak[row] = top
                total[row] = total[row] * shrink + summed
                acc[row] = acc[row] * shrink + product
        return carry

    lax.fori_loop(0, turns(table, range(ROWS)), step, 0)
    for row in range(ROWS):
        unit, i = row // NBLK, row % NBLK
        lse_ref[unit, i] = peak[row] + jnp.log2(total[row])
        dq_ref[unit, i] = (acc[row] * (SCALE / total[row])).T.astype(jnp.bfloat16)


def flat(array):
    return array.reshape((ENTRIES,) + array.shape[3:])


def query_pass(table, query_own, grad_own, delta, key, value, peak, total, acc):
    return pl.pallas_call(
        query_kernel,
        out_shape=(jax.ShapeDtypeStruct(OWN, jnp.bfloat16), jax.ShapeDtypeStruct((2, NBLK, 1, BLK), jnp.float32)),
        in_specs=[SMEM] + [VMEM] * 8,
        out_specs=(VMEM, VMEM),
        scratch_shapes=[
            pltpu.VMEM((ROWS, 1, BLK), jnp.float32),
            pltpu.VMEM((ROWS, 1, BLK), jnp.float32),
            pltpu.VMEM((ROWS, HEAD_DIM, BLK), jnp.float32),
        ],
        compiler_params=pltpu.CompilerParams(vmem_limit_bytes=LIMIT),
        name="query_pass",
    )(table, query_own, grad_own, delta, flat(key), flat(value), peak, total, acc)


def share_kernel(lse_own, delta_all, query_own, grad_own, key_all, value_all, grad_part, lse_all, grad_all,
                 key_acc, value_acc, send, recv, send2, recv2, load):
    ring = Ring()
    member = ring.member

    barrier = pltpu.get_barrier_semaphore()
    for step in range(1, GROUP):
        slot = (member + step) % GROUP
        pl.semaphore_signal(barrier, inc=1, device_id=ring.device(slot), device_id_type=MESH)
    pl.semaphore_wait(barrier, GROUP - 1)
    pending = []
    for step in range(1, GROUP):
        device = ring.device((member + step) % GROUP)
        pending.append(remote(lse_own, lse_all.at[:, member], send.at[step], recv.at[step], device))
    mine = pltpu.make_async_copy(lse_own, lse_all.at[:, member], load.at[6])
    mine.start()
    pending.append(
        remote(grad_part.at[0, ring.down], grad_all.at[0, ring.down], send2.at[0], recv2.at[0], ring.device(ring.up))
    )
    pending.append(
        remote(grad_part.at[1, ring.up], grad_all.at[1, ring.up], send2.at[1], recv2.at[1], ring.device(ring.down))
    )
    held = (ring.member, ring.up, ring.down, ring.twin, ring.twin_up, ring.twin_down)
    loads = []
    for n, slot in enumerate(held):
        loads.append(pltpu.make_async_copy(grad_part.at[:, slot], grad_all.at[:, slot], load.at[n]))
        loads[-1].start()

    def relay(n):
        part = grad_all.at[n, ring.far]
        arrived(part, recv2.at[n])
        pending.append(remote(part, part, send2.at[2 + n], recv2.at[2 + n], ring.device(ring.twin)))

    for unit in range(2):
        query = query_own[unit].reshape(NBLK * BLK, HEAD_DIM)
        grad = grad_own[unit].reshape(NBLK * BLK, HEAD_DIM)
        delta = jnp.concatenate([delta_all[unit, member, i] for i in range(NBLK)], axis=1)
        lse = jnp.concatenate([lse_own[unit, i] for i in range(NBLK)], axis=1)
        span = WIDE // BLK
        for u in range(0, NBLK, span):
            key = key_all[unit, member, u : u + span].reshape(WIDE, HEAD_DIM)
            value = value_all[unit, member, u : u + span].reshape(WIDE, HEAD_DIM)
            probs = jnp.exp2(dot(key, query, NT) * SCALE2 - lse)
            terms = (probs * (dot(value, grad, NT) - delta)).astype(jnp.bfloat16)
            value_part = dot(probs.astype(jnp.bfloat16), grad)
            key_part = dot(terms, query)
            for s in range(span):
                rows = slice(s * BLK, (s + 1) * BLK)
                value_acc[unit * NBLK + u + s] = value_part[rows]
                key_acc[unit * NBLK + u + s] = key_part[rows]

    relay(0)
    relay(1)
    mine.wait()
    for copy in loads:
        copy.wait()
    for step in range(1, GROUP):
        arrived(lse_own, recv.at[step])
    arrived(grad_all.at[0, ring.twin_far], recv2.at[2])
    arrived(grad_all.at[1, ring.twin_far], recv2.at[3])
    for copy in pending:
        copy.wait_send()


def share_totals(lse_own, delta, query_own, grad_own, key, value, grad):
    return pl.pallas_call(
        share_kernel,
        out_shape=(
            jax.ShapeDtypeStruct(STATS, jnp.float32),
            jax.ShapeDtypeStruct(WHOLE, jnp.bfloat16),
            jax.ShapeDtypeStruct((ROWS, BLK, HEAD_DIM), jnp.float32),
            jax.ShapeDtypeStruct((ROWS, BLK, HEAD_DIM), jnp.float32),
        ),
        in_specs=[VMEM] * 6 + [ANY],
        out_specs=(VMEM,) * 4,
        scratch_shapes=[
            pltpu.SemaphoreType.DMA((GROUP,)),
            pltpu.SemaphoreType.DMA((GROUP,)),
            pltpu.SemaphoreType.DMA((4,)),
            pltpu.SemaphoreType.DMA((4,)),
            pltpu.SemaphoreType.DMA((7,)),
        ],
        compiler_params=pltpu.CompilerParams(collective_id=1, has_side_effects=True, vmem_limit_bytes=LIMIT),
        name="share_totals",
    )(lse_own, delta, query_own, grad_own, key, value, grad)


def key_kernel(other, table, key_all, value_all, delta_ref, lse_ref, query_ref, grad_ref, key_in, value_in, out_ref,
               key_acc, value_acc):
    _, half, member = place()
    unit = 1 - half if other else half
    base = unit * NBLK
    for u in range(NBLK):
        key_acc[u] = key_in[base + u]
        value_acc[u] = value_in[base + u]

    def step(turn, carry):
        for first in range(0, NBLK, PAIR):
            blocks = range(first, first + PAIR)
            loads, results = [], []
            for u in blocks:
                row = base + u
                slots = [turn * CHUNK + c for c in range(CHUNK)]
                entries = [table[row, slot] for slot in slots]
                bias = [jnp.where(slot < table[row, COUNT_AT], 0.0, FAR) for slot in slots]
                query = jnp.concatenate([query_ref[e] for e in entries], axis=0)
                grad = jnp.concatenate([grad_ref[e] for e in entries], axis=0)
                lse = jnp.concatenate([lse_ref[e] + b for e, b in zip(entries, bias)], axis=1)
                delta = jnp.concatenate([delta_ref[e] for e in entries], axis=1)
                scores = dot(key_all[unit, member, u], query, NT)
                grads = dot(value_all[unit, member, u], grad, NT)
                loads.append((query, grad, lse, delta, scores, grads))
            for query, grad, lse, delta, scores, grads in loads:
                probs = jnp.exp2(scores * SCALE2 - lse)
                terms = (probs * (grads - delta)).astype(jnp.bfloat16)
                results.append((dot(probs.astype(jnp.bfloat16), grad), dot(terms, query)))
            for n, u in enumerate(blocks):
                value_acc[u] += results[n][0]
                key_acc[u] += results[n][1]
        return carry

    lax.fori_loop(0, turns(table, [base + u for u in range(NBLK)]), step, 0)
    for u in range(NBLK):
        out_ref[0, u] = (key_acc[u] * SCALE).astype(jnp.bfloat16)
        out_ref[1, u] = value_acc[u].astype(jnp.bfloat16)


def key_pass(other, table, key, value, delta, lse, query, grad, key_acc, value_acc):
    def kernel(*refs):
        key_kernel(other, *refs)

    return pl.pallas_call(
        kernel,
        out_shape=jax.ShapeDtypeStruct(OWN, jnp.bfloat16),
        in_specs=[SMEM] + [VMEM] * 8,
        out_specs=VMEM,
        scratch_shapes=[
            pltpu.VMEM((NBLK, BLK, HEAD_DIM), jnp.float32),
            pltpu.VMEM((NBLK, BLK, HEAD_DIM), jnp.float32),
        ],
        compiler_params=pltpu.CompilerParams(vmem_limit_bytes=LIMIT),
        cost_estimate=pl.CostEstimate(flops=2_000_000_000, bytes_accessed=1 << 20, transcendentals=1 << 20),
        name="key_pass_sent" if other else "key_pass_kept",
    )(table, key, value, flat(delta), flat(lse), flat(query), flat(grad), key_acc, value_acc)


def local(queries, key_states, value_states, attn_out, grad_out, frame_order, block_live):
    half = place()[1]
    (key, value, query, grad, delta, query_own, grad_own, peak, total, acc, by_query, by_key) = gather_all(
        frame_order, block_live, key_states, value_states, queries, grad_out, attn_out
    )
    dq, lse_own = query_pass(by_query, query_own, grad_own, delta, key, value, peak, total, acc)
    swap = [(source, (source + GROUP) % (2 * GROUP)) for source in range(2 * GROUP)]

    def across(sent):
        return lax.ppermute(sent, "frame", swap)

    def join(kept, came):
        kept, came = kept.reshape(NBLK * BLK, HEAD_DIM), came.reshape(NBLK * BLK, HEAD_DIM)
        return jnp.concatenate([jnp.where(half == 0, kept, came), jnp.where(half == 0, came, kept)], axis=1)

    dq_came = across(jnp.where(half == 0, dq[1], dq[0]))
    lse, grad, key_acc, value_acc = share_totals(lse_own, delta, query_own, grad_own, key, value, grad)
    sums = (by_key, key, value, delta, lse, query, grad, key_acc, value_acc)
    came = across(key_pass(True, *sums))
    kept = key_pass(False, *sums)
    return join(jnp.where(half == 0, dq[0], dq[1]), dq_came), join(kept[0], came[0]), join(kept[1], came[1])


def solution(mesh):
    rows = P(("frame", "head"), None)
    out = P("frame", "head")
    return jax.shard_map(
        local,
        mesh=mesh,
        in_specs=(rows, rows, rows, rows, rows, P(), P()),
        out_specs=(out, out, out),
        check_vma=False,
    )
```

```python
import math

import jax
import jax.numpy as jnp
from jax import lax
from jax.experimental import pallas as pl
from jax.experimental.pallas import tpu as pltpu
from jax.sharding import PartitionSpec as P

HEADS = 16
HEAD_DIM = 128
SCALE = HEAD_DIM ** (-0.5)
SCALE2 = SCALE * math.log2(math.e)
REACH = 4
NBLK = 8
BLK = 128
RING = 4
GROUP = 8
ROWS = 2 * NBLK
ENTRIES = 2 * GROUP * NBLK
SLOTS = 2 * (REACH - 1) * NBLK
COUNT_AT = BLK - 1
CHUNK = 5
PAIR = 2
WIDE = 512
FAR = 1e30
MESH = pl.DeviceIdType.MESH
ANY = pl.BlockSpec(memory_space=pl.ANY)
SMEM = pl.BlockSpec(memory_space=pltpu.SMEM)
HBM = pl.BlockSpec(memory_space=pltpu.HBM)
VMEM = pl.BlockSpec(memory_space=pltpu.VMEM)
NN = (((1,), (0,)), ((), ()))
NT = (((1,), (1,)), ((), ()))
TN = (((0,), (0,)), ((), ()))
KEY, VALUE, QUERY, GRAD, DELTA = range(5)


def dot(a, b, dims=NN):
    return lax.dot_general(a, b, dims, preferred_element_type=jnp.float32)


def place():
    frame = lax.axis_index("frame")
    return lax.axis_index("head"), frame // GROUP, frame % GROUP


class Ring:
    def __init__(self):
        self.head, self.half, self.member = place()
        ring, core = self.member // 2, self.member % 2
        up, down, far = (ring + 1) % RING, (ring + RING - 1) % RING, (ring + 2) % RING
        self.up, self.down, self.far = up * 2 + core, down * 2 + core, far * 2 + core
        self.twin = ring * 2 + 1 - core
        self.twin_up, self.twin_down, self.twin_far = up * 2 + 1 - core, down * 2 + 1 - core, far * 2 + 1 - core

    def device(self, slot):
        return {"head": self.head, "frame": self.half * GROUP + slot}


def remote(src, dst, send, recv, device):
    copy = pltpu.make_async_remote_copy(
        src_ref=src, dst_ref=dst, send_sem=send, recv_sem=recv, device_id=device, device_id_type=MESH
    )
    copy.start()
    return copy


def arrived(part, sem):
    pltpu.make_async_copy(part, part, sem).wait()


def live_list(flags):
    spot = lax.broadcasted_iota(jnp.int32, (ENTRIES, ENTRIES), 0)
    later = lax.broadcasted_iota(jnp.int32, (ENTRIES, ENTRIES), 1)
    before = jnp.where(spot < later, 1.0, 0.0).astype(jnp.bfloat16)
    ahead = dot(flags.astype(jnp.bfloat16), before)
    lane = lax.broadcasted_iota(jnp.int32, (ROWS, ENTRIES), 1)
    value = lane.astype(jnp.float32) * flags
    ahead = jnp.where(flags > 0.0, ahead, -1.0)
    table = jnp.where(lane == COUNT_AT, jnp.sum(flags, axis=1, keepdims=True), 0.0)
    for k in range(SLOTS):
        found = jnp.sum(jnp.where(ahead == float(k), value, 0.0), axis=1, keepdims=True)
        table = jnp.where(lane == k, found, table)
    return table.astype(jnp.int32)


def write_tables(member, order_ref, live_ref, by_query_ref, by_key_ref):
    lane = lax.broadcasted_iota(jnp.int32, (1, ENTRIES), 1)
    order = jnp.zeros((1, ENTRIES), jnp.int32)
    for g in range(2 * GROUP):
        order = jnp.where(lane // NBLK == g, order_ref[g], order)
    rows = lax.broadcasted_iota(jnp.int32, (NBLK, ENTRIES), 0)
    lanes = lax.broadcasted_iota(jnp.int32, (NBLK, ENTRIES), 1)
    spread = jnp.where(lanes % NBLK == rows, 1.0, 0.0).astype(jnp.bfloat16)
    query_rows, key_rows = [], []
    for unit in range(2):
        distance = jnp.abs(order - order_ref[unit * GROUP + member])
        by_query = jnp.zeros((NBLK, ENTRIES), jnp.float32)
        by_key = jnp.zeros((NBLK, ENTRIES), jnp.float32)
        for d in range(1, REACH):
            blocks = live_ref[d].astype(jnp.float32).astype(jnp.bfloat16)
            here = distance == d
            by_query = jnp.where(here, dot(blocks, spread), by_query)
            by_key = jnp.where(here, dot(blocks, spread, TN), by_key)
        query_rows.append(by_query)
        key_rows.append(by_key)
    by_query_ref[...] = live_list(jnp.concatenate(query_rows, axis=0))
    by_key_ref[...] = live_list(jnp.concatenate(key_rows, axis=0))


def gather_kernel(order_src, live_src, out_src, key_src, value_src, query_src, grad_src, key_all, value_all, query_all,
                  grad_all, delta_all, query_own, grad_own, peak, total, acc, by_query_ref, by_key_ref, delta_src, raw,
                  grad_raw, out_raw, order_ref, live_ref, send1, recv1, send2, recv2, send3, recv3, load):
    ring = Ring()
    head, half, member = ring.head, ring.half, ring.member
    plane = head * 2 + half
    srcs = (key_src, value_src, query_src, grad_src, delta_src)
    bufs = (key_all, value_all, query_all, grad_all, delta_all)

    def plane_peer(step):
        other = (plane + step) % HEADS
        return other, {"head": other // 2, "frame": (other % 2) * GROUP + member}

    fetches = [
        pltpu.make_async_copy(grad_src, grad_raw, load.at[0]),
        pltpu.make_async_copy(out_src, out_raw, load.at[1]),
        pltpu.make_async_copy(order_src, order_ref, load.at[2]),
        pltpu.make_async_copy(live_src, live_ref, load.at[3]),
    ]
    for fetch in fetches:
        fetch.start()
    barrier = pltpu.get_barrier_semaphore()
    for step in range(1, HEADS):
        pl.semaphore_signal(barrier, inc=1, device_id=plane_peer(step)[1], device_id_type=MESH)
    for slot in (ring.up, ring.down, ring.twin):
        pl.semaphore_signal(barrier, inc=1, device_id=ring.device(slot), device_id_type=MESH)
    pl.semaphore_wait(barrier, HEADS - 1 + 3)

    pending = []
    pending.append(remote(query_src, raw.at[0], send3.at[0], recv3.at[0], ring.device(ring.up)))
    pending.append(remote(query_src, raw.at[1], send3.at[1], recv3.at[1], ring.device(ring.down)))

    def column(src, other):
        if src is delta_src:
            return src.at[other]
        return src.at[:, pl.ds(pl.multiple_of(other * HEAD_DIM, HEAD_DIM), HEAD_DIM)]

    def scatter(src, target, send, recv):
        for step in range(1, HEADS):
            other, device = plane_peer(step)
            remote(column(src, other), target, send, recv, device)
        pltpu.make_async_copy(column(src, plane), target, recv).start()

    for a in (KEY, VALUE, QUERY, GRAD):
        scatter(srcs[a], bufs[a].at[half, member, head], send1.at[a], recv1.at[a])
    fetches[0].wait()
    fetches[1].wait()
    for n in range(HEADS):
        lanes = slice(n * HEAD_DIM, (n + 1) * HEAD_DIM)
        products = grad_raw[:, lanes].astype(jnp.float32) * out_raw[:, lanes].astype(jnp.float32)
        delta_src[n] = jnp.sum(products.T, axis=0, keepdims=True)
    scatter(delta_src, bufs[DELTA].at[half, member, head], send1.at[DELTA], recv1.at[DELTA])

    def push(a, number, part, slot, arrive):
        pending.append(remote(part, part, send2.at[a, number], recv2.at[a, arrive], ring.device(slot)))

    def spread(a):
        own = bufs[a].at[:, member]
        arrived(own, recv1.at[a])
        if a != QUERY:
            push(a, 0, own, ring.up, 0)
            push(a, 1, own, ring.down, 1)
        push(a, 2, own, ring.twin, 4)

    def pass_raw(number, slot):
        scatter(raw.at[number], bufs[QUERY].at[half, slot, head], send1.at[5 + number], recv1.at[5 + number])

    upper, lower = pl.ds(0, BLK // 2), pl.ds(BLK // 2, BLK // 2)
    spread(KEY)
    fetches[2].wait()
    fetches[3].wait()
    write_tables(member, order_ref, live_ref, by_query_ref, by_key_ref)
    spread(VALUE)
    arrived(raw.at[0], recv3.at[0])
    pending.append(remote(raw.at[0, upper], raw.at[2, upper], send3.at[2], recv3.at[2], ring.device(ring.up)))
    pass_raw(0, ring.down)
    arrived(raw.at[1], recv3.at[1])
    pending.append(remote(raw.at[1, lower], raw.at[2, lower], send3.at[3], recv3.at[3], ring.device(ring.down)))
    pass_raw(1, ring.up)
    spread(QUERY)
    fetch_query = pltpu.make_async_copy(bufs[QUERY].at[:, member], query_own, load.at[4])
    fetch_query.start()
    spread(GRAD)
    fetch_grad = pltpu.make_async_copy(bufs[GRAD].at[:, member], grad_own, load.at[5])
    fetch_grad.start()
    spread(DELTA)
    fetch_query.wait()
    fetch_grad.wait()

    span = WIDE // BLK
    for unit in range(2):
        key = key_all[unit, member].reshape(NBLK * BLK, HEAD_DIM)
        value = value_all[unit, member].reshape(NBLK * BLK, HEAD_DIM)
        for i in range(0, NBLK, span):
            query = query_own[unit, i : i + span].reshape(WIDE, HEAD_DIM)
            grad = grad_own[unit, i : i + span].reshape(WIDE, HEAD_DIM)
            delta = jnp.concatenate([delta_all[unit, member, i + s] for s in range(span)], axis=1)
            scores = dot(key, query, NT) * SCALE2
            top = jnp.max(scores, axis=0, keepdims=True)
            probs = jnp.exp2(scores - top)
            summed = jnp.sum(probs, axis=0, keepdims=True)
            terms = (probs * (dot(value, grad, NT) - delta)).astype(jnp.bfloat16)
            partial = dot(key, terms, TN)
            for s in range(span):
                lanes = slice(s * BLK, (s + 1) * BLK)
                row = unit * NBLK + i + s
                peak[row] = top[:, lanes]
                total[row] = summed[:, lanes]
                acc[row] = partial[:, lanes]

    arrived(raw.at[2, upper], recv3.at[2])
    arrived(raw.at[2, lower], recv3.at[3])
    pass_raw(2, ring.far)
    arrived(bufs[QUERY].at[:, ring.down], recv1.at[5])
    push(QUERY, 4, bufs[QUERY].at[:, ring.down], ring.twin, 5)
    arrived(bufs[QUERY].at[:, ring.up], recv1.at[6])
    push(QUERY, 6, bufs[QUERY].at[:, ring.up], ring.twin, 6)
    for a in (KEY, VALUE, GRAD, DELTA):
        part = bufs[a].at[:, ring.down]
        arrived(part, recv2.at[a, 0])
        if a != GRAD:
            push(a, 3, bufs[a].at[0, ring.down], ring.up, 2)
        push(a, 4, part, ring.twin, 5)
        part = bufs[a].at[:, ring.up]
        arrived(part, recv2.at[a, 1])
        if a != GRAD:
            push(a, 5, bufs[a].at[1, ring.up], ring.down, 3)
        push(a, 6, part, ring.twin, 6)
    arrived(bufs[QUERY].at[:, ring.far], recv1.at[7])
    push(QUERY, 7, bufs[QUERY].at[:, ring.far], ring.twin, 7)
    for a in (KEY, VALUE, DELTA):
        part = bufs[a].at[0, ring.far]
        arrived(part, recv2.at[a, 2])
        push(a, 7, part, ring.twin, 7)
        part = bufs[a].at[1, ring.far]
        arrived(part, recv2.at[a, 3])
        push(a, 8, part, ring.twin, 8)
    for a in (KEY, VALUE, QUERY, GRAD, DELTA):
        arrived(bufs[a].at[:, ring.twin], recv2.at[a, 4])
        arrived(bufs[a].at[:, ring.twin_down], recv2.at[a, 5])
        arrived(bufs[a].at[:, ring.twin_up], recv2.at[a, 6])
        if a == QUERY:
            arrived(bufs[a].at[:, ring.twin_far], recv2.at[a, 7])
        elif a != GRAD:
            arrived(bufs[a].at[0, ring.twin_far], recv2.at[a, 7])
            arrived(bufs[a].at[1, ring.twin_far], recv2.at[a, 8])
    for copy in pending:
        copy.wait_send()
    for a in range(8):
        source = srcs[a] if a < 5 else raw.at[a - 5]
        sent = source.at[pl.ds(0, HEADS - 1)] if a == DELTA else source.at[:, pl.ds(0, (HEADS - 1) * HEAD_DIM)]
        arrived(sent, send1.at[a])


WHOLE = (2, GROUP, NBLK, BLK, HEAD_DIM)
STATS = (2, GROUP, NBLK, 1, BLK)
OWN = (2, NBLK, BLK, HEAD_DIM)
LIMIT = 24 << 20


def gather_all(order, live, key, value, query, grad, out):
    low, full, whole = jnp.bfloat16, jnp.float32, jnp.int32
    return pl.pallas_call(
        gather_kernel,
        out_shape=(
            jax.ShapeDtypeStruct(WHOLE, low),
            jax.ShapeDtypeStruct(WHOLE, low),
            jax.ShapeDtypeStruct(WHOLE, low),
            jax.ShapeDtypeStruct(WHOLE, low),
            jax.ShapeDtypeStruct(STATS, full),
            jax.ShapeDtypeStruct(OWN, low),
            jax.ShapeDtypeStruct(OWN, low),
            jax.ShapeDtypeStruct((ROWS, 1, BLK), full),
            jax.ShapeDtypeStruct((ROWS, 1, BLK), full),
            jax.ShapeDtypeStruct((ROWS, HEAD_DIM, BLK), full),
            jax.ShapeDtypeStruct((ROWS, ENTRIES), whole),
            jax.ShapeDtypeStruct((ROWS, ENTRIES), whole),
        ),
        in_specs=[HBM] * 7,
        out_specs=(VMEM, VMEM, VMEM, ANY) + (VMEM,) * 8,
        scratch_shapes=[
            pltpu.VMEM((HEADS, 1, BLK), full),
            pltpu.VMEM((3, BLK, HEADS * HEAD_DIM), low),
            pltpu.VMEM((BLK, HEADS * HEAD_DIM), low),
            pltpu.VMEM((BLK, HEADS * HEAD_DIM), low),
            pltpu.SMEM((2 * GROUP,), whole),
            pltpu.VMEM((2 * GROUP, NBLK, NBLK), whole),
            pltpu.SemaphoreType.DMA((8,)),
            pltpu.SemaphoreType.DMA((8,)),
            pltpu.SemaphoreType.DMA((5, 9)),
            pltpu.SemaphoreType.DMA((5, 9)),
            pltpu.SemaphoreType.DMA((4,)),
            pltpu.SemaphoreType.DMA((4,)),
            pltpu.SemaphoreType.DMA((6,)),
        ],
        compiler_params=pltpu.CompilerParams(collective_id=0, has_side_effects=True, vmem_limit_bytes=LIMIT),
        name="gather_all",
    )(*(pltpu.with_memory_space_constraint(x, pltpu.HBM) for x in (order, live, out, key, value, query, grad)))


def turns(table, rows):
    most = table[rows[0], COUNT_AT]
    for row in rows[1:]:
        most = jnp.maximum(most, table[row, COUNT_AT])
    return (most + CHUNK - 1) // CHUNK


def query_kernel(table, query_own, grad_own, delta_all, key_ref, value_ref, peak_in, total_in, acc_in, dq_ref, lse_ref,
                 peak, total, acc):
    member = place()[2]
    peak[...] = peak_in[...]
    total[...] = total_in[...]
    acc[...] = acc_in[...]

    def step(turn, carry):
        for first in range(0, ROWS, PAIR):
            rows = range(first, first + PAIR)
            keys, scores, grads = [], [], []
            for row in rows:
                unit, i = row // NBLK, row % NBLK
                slots = [turn * CHUNK + c for c in range(CHUNK)]
                entries = [table[row, slot] for slot in slots]
                bias = [jnp.where(slot < table[row, COUNT_AT], 0.0, -FAR) for slot in slots]
                key = jnp.concatenate([key_ref[e] for e in entries], axis=0)
                value = jnp.concatenate([value_ref[e] for e in entries], axis=0)
                s = dot(key, query_own[unit, i], NT)
                s = jnp.concatenate([s[c * BLK : (c + 1) * BLK] * SCALE2 + bias[c] for c in range(CHUNK)], axis=0)
                keys.append(key)
                scores.append(s)
                grads.append(dot(value, grad_own[unit, i], NT) - delta_all[unit, member, i])
            results = []
            for n, row in enumerate(rows):
                before = peak[row]
                top = jnp.maximum(before, jnp.max(scores[n], axis=0, keepdims=True))
                probs = jnp.exp2(scores[n] - top)
                terms = (probs * grads[n]).astype(jnp.bfloat16)
                results.append((top, jnp.exp2(before - top), jnp.sum(probs, axis=0, keepdims=True), dot(keys[n], terms, TN)))
            for n, row in enumerate(rows):
                top, shrink, summed, product = results[n]
                peak[row] = top
                total[row] = total[row] * shrink + summed
                acc[row] = acc[row] * shrink + product
        return carry

    lax.fori_loop(0, turns(table, range(ROWS)), step, 0)
    for row in range(ROWS):
        unit, i = row // NBLK, row % NBLK
        lse_ref[unit, i] = peak[row] + jnp.log2(total[row])
        dq_ref[unit, i] = (acc[row] * (SCALE / total[row])).T.astype(jnp.bfloat16)


def flat(array):
    return array.reshape((ENTRIES,) + array.shape[3:])


def query_pass(table, query_own, grad_own, delta, key, value, peak, total, acc):
    return pl.pallas_call(
        query_kernel,
        out_shape=(jax.ShapeDtypeStruct(OWN, jnp.bfloat16), jax.ShapeDtypeStruct((2, NBLK, 1, BLK), jnp.float32)),
        in_specs=[SMEM] + [VMEM] * 8,
        out_specs=(VMEM, VMEM),
        scratch_shapes=[
            pltpu.VMEM((ROWS, 1, BLK), jnp.float32),
            pltpu.VMEM((ROWS, 1, BLK), jnp.float32),
            pltpu.VMEM((ROWS, HEAD_DIM, BLK), jnp.float32),
        ],
        compiler_params=pltpu.CompilerParams(vmem_limit_bytes=LIMIT),
        name="query_pass",
    )(table, query_own, grad_own, delta, flat(key), flat(value), peak, total, acc)


def share_kernel(lse_own, delta_all, query_own, grad_own, key_all, value_all, grad_part, lse_all, grad_all,
                 key_acc, value_acc, send, recv, send2, recv2, load):
    ring = Ring()
    member = ring.member

    barrier = pltpu.get_barrier_semaphore()
    for step in range(1, GROUP):
        slot = (member + step) % GROUP
        pl.semaphore_signal(barrier, inc=1, device_id=ring.device(slot), device_id_type=MESH)
    pl.semaphore_wait(barrier, GROUP - 1)
    pending = []
    for step in range(1, GROUP):
        device = ring.device((member + step) % GROUP)
        pending.append(remote(lse_own, lse_all.at[:, member], send.at[step], recv.at[step], device))
    mine = pltpu.make_async_copy(lse_own, lse_all.at[:, member], load.at[6])
    mine.start()
    pending.append(
        remote(grad_part.at[0, ring.down], grad_all.at[0, ring.down], send2.at[0], recv2.at[0], ring.device(ring.up))
    )
    pending.append(
        remote(grad_part.at[1, ring.up], grad_all.at[1, ring.up], send2.at[1], recv2.at[1], ring.device(ring.down))
    )
    held = (ring.member, ring.up, ring.down, ring.twin, ring.twin_up, ring.twin_down)
    loads = []
    for n, slot in enumerate(held):
        loads.append(pltpu.make_async_copy(grad_part.at[:, slot], grad_all.at[:, slot], load.at[n]))
        loads[-1].start()

    def relay(n):
        part = grad_all.at[n, ring.far]
        arrived(part, recv2.at[n])
        pending.append(remote(part, part, send2.at[2 + n], recv2.at[2 + n], ring.device(ring.twin)))

    for unit in range(2):
        query = query_own[unit].reshape(NBLK * BLK, HEAD_DIM)
        grad = grad_own[unit].reshape(NBLK * BLK, HEAD_DIM)
        delta = jnp.concatenate([delta_all[unit, member, i] for i in range(NBLK)], axis=1)
        lse = jnp.concatenate([lse_own[unit, i] for i in range(NBLK)], axis=1)
        span = WIDE // BLK
        for u in range(0, NBLK, span):
            key = key_all[unit, member, u : u + span].reshape(WIDE, HEAD_DIM)
            value = value_all[unit, member, u : u + span].reshape(WIDE, HEAD_DIM)
            probs = jnp.exp2(dot(key, query, NT) * SCALE2 - lse)
            terms = (probs * (dot(value, grad, NT) - delta)).astype(jnp.bfloat16)
            value_part = dot(probs.astype(jnp.bfloat16), grad)
            key_part = dot(terms, query)
            for s in range(span):
                rows = slice(s * BLK, (s + 1) * BLK)
                value_acc[unit * NBLK + u + s] = value_part[rows]
                key_acc[unit * NBLK + u + s] = key_part[rows]

    relay(0)
    relay(1)
    mine.wait()
    for copy in loads:
        copy.wait()
    for step in range(1, GROUP):
        arrived(lse_own, recv.at[step])
    arrived(grad_all.at[0, ring.twin_far], recv2.at[2])
    arrived(grad_all.at[1, ring.twin_far], recv2.at[3])
    for copy in pending:
        copy.wait_send()


def share_totals(lse_own, delta, query_own, grad_own, key, value, grad):
    return pl.pallas_call(
        share_kernel,
        out_shape=(
            jax.ShapeDtypeStruct(STATS, jnp.float32),
            jax.ShapeDtypeStruct(WHOLE, jnp.bfloat16),
            jax.ShapeDtypeStruct((ROWS, BLK, HEAD_DIM), jnp.float32),
            jax.ShapeDtypeStruct((ROWS, BLK, HEAD_DIM), jnp.float32),
        ),
        in_specs=[VMEM] * 6 + [ANY],
        out_specs=(VMEM,) * 4,
        scratch_shapes=[
            pltpu.SemaphoreType.DMA((GROUP,)),
            pltpu.SemaphoreType.DMA((GROUP,)),
            pltpu.SemaphoreType.DMA((4,)),
            pltpu.SemaphoreType.DMA((4,)),
            pltpu.SemaphoreType.DMA((7,)),
        ],
        compiler_params=pltpu.CompilerParams(collective_id=1, has_side_effects=True, vmem_limit_bytes=LIMIT),
        name="share_totals",
    )(lse_own, delta, query_own, grad_own, key, value, grad)


def key_kernel(other, table, key_all, value_all, delta_ref, lse_ref, query_ref, grad_ref, key_in, value_in, out_ref,
               key_acc, value_acc):
    _, half, member = place()
    unit = 1 - half if other else half
    base = unit * NBLK
    for u in range(NBLK):
        key_acc[u] = key_in[base + u]
        value_acc[u] = value_in[base + u]

    def step(turn, carry):
        for first in range(0, NBLK, PAIR):
            blocks = range(first, first + PAIR)
            loads, results = [], []
            for u in blocks:
                row = base + u
                slots = [turn * CHUNK + c for c in range(CHUNK)]
                entries = [table[row, slot] for slot in slots]
                bias = [jnp.where(slot < table[row, COUNT_AT], 0.0, FAR) for slot in slots]
                query = jnp.concatenate([query_ref[e] for e in entries], axis=0)
                grad = jnp.concatenate([grad_ref[e] for e in entries], axis=0)
                lse = jnp.concatenate([lse_ref[e] + b for e, b in zip(entries, bias)], axis=1)
                delta = jnp.concatenate([delta_ref[e] for e in entries], axis=1)
                scores = dot(key_all[unit, member, u], query, NT)
                grads = dot(value_all[unit, member, u], grad, NT)
                loads.append((query, grad, lse, delta, scores, grads))
            for query, grad, lse, delta, scores, grads in loads:
                probs = jnp.exp2(scores * SCALE2 - lse)
                terms = (probs * (grads - delta)).astype(jnp.bfloat16)
                results.append((dot(probs.astype(jnp.bfloat16), grad), dot(terms, query)))
            for n, u in enumerate(blocks):
                value_acc[u] += results[n][0]
                key_acc[u] += results[n][1]
        return carry

    lax.fori_loop(0, turns(table, [base + u for u in range(NBLK)]), step, 0)
    for u in range(NBLK):
        out_ref[0, u] = (key_acc[u] * SCALE).astype(jnp.bfloat16)
        out_ref[1, u] = value_acc[u].astype(jnp.bfloat16)


def key_pass(other, table, key, value, delta, lse, query, grad, key_acc, value_acc):
    def kernel(*refs):
        key_kernel(other, *refs)

    return pl.pallas_call(
        kernel,
        out_shape=jax.ShapeDtypeStruct(OWN, jnp.bfloat16),
        in_specs=[SMEM] + [VMEM] * 8,
        out_specs=VMEM,
        scratch_shapes=[
            pltpu.VMEM((NBLK, BLK, HEAD_DIM), jnp.float32),
            pltpu.VMEM((NBLK, BLK, HEAD_DIM), jnp.float32),
        ],
        compiler_params=pltpu.CompilerParams(vmem_limit_bytes=LIMIT),
        cost_estimate=pl.CostEstimate(flops=2_000_000_000, bytes_accessed=1 << 20, transcendentals=1 << 20),
        name="key_pass_sent" if other else "key_pass_kept",
    )(table, key, value, flat(delta), flat(lse), flat(query), flat(grad), key_acc, value_acc)


def local(queries, key_states, value_states, attn_out, grad_out, frame_order, block_live):
    half = place()[1]
    (key, value, query, grad, delta, query_own, grad_own, peak, total, acc, by_query, by_key) = gather_all(
        frame_order, block_live, key_states, value_states, queries, grad_out, attn_out
    )
    dq, lse_own = query_pass(by_query, query_own, grad_own, delta, key, value, peak, total, acc)
    swap = [(source, (source + GROUP) % (2 * GROUP)) for source in range(2 * GROUP)]

    def across(sent):
        return lax.ppermute(sent, "frame", swap)

    def join(kept, came):
        kept, came = kept.reshape(NBLK * BLK, HEAD_DIM), came.reshape(NBLK * BLK, HEAD_DIM)
        return jnp.concatenate([jnp.where(half == 0, kept, came), jnp.where(half == 0, came, kept)], axis=1)

    dq_came = across(jnp.where(half == 0, dq[1], dq[0]))
    lse, grad, key_acc, value_acc = share_totals(lse_own, delta, query_own, grad_own, key, value, grad)
    sums = (by_key, key, value, delta, lse, query, grad, key_acc, value_acc)
    came = across(key_pass(True, *sums))
    kept = key_pass(False, *sums)
    return join(jnp.where(half == 0, dq[0], dq[1]), dq_came), join(kept[0], came[0]), join(kept[1], came[1])


def solution(mesh):
    rows = P(("frame", "head"), None)
    out = P("frame", "head")
    return jax.shard_map(
        local,
        mesh=mesh,
        in_specs=(rows, rows, rows, rows, rows, P(), P()),
        out_specs=(out, out, out),
        check_vma=False,
    )
```

```python
import math

import jax
import jax.numpy as jnp
from jax import lax
from jax.experimental import pallas as pl
from jax.experimental.pallas import tpu as pltpu
from jax.sharding import PartitionSpec as P

HEADS = 16
HEAD_DIM = 128
SCALE = HEAD_DIM ** (-0.5)
SCALE2 = SCALE * math.log2(math.e)
REACH = 4
NBLK = 8
BLK = 128
RING = 4
GROUP = 8
ROWS = 2 * NBLK
ENTRIES = 2 * GROUP * NBLK
SLOTS = 2 * (REACH - 1) * NBLK
COUNT_AT = BLK - 1
CHUNK = 5
PAIR = 2
WIDE = 512
FAR = 1e30
MESH = pl.DeviceIdType.MESH
ANY = pl.BlockSpec(memory_space=pl.ANY)
SMEM = pl.BlockSpec(memory_space=pltpu.SMEM)
HBM = pl.BlockSpec(memory_space=pltpu.HBM)
VMEM = pl.BlockSpec(memory_space=pltpu.VMEM)
NN = (((1,), (0,)), ((), ()))
NT = (((1,), (1,)), ((), ()))
TN = (((0,), (0,)), ((), ()))
KEY, VALUE, QUERY, GRAD, DELTA = range(5)


def dot(a, b, dims=NN):
    return lax.dot_general(a, b, dims, preferred_element_type=jnp.float32)


def place():
    frame = lax.axis_index("frame")
    return lax.axis_index("head"), frame // GROUP, frame % GROUP


class Ring:
    def __init__(self):
        self.head, self.half, self.member = place()
        ring, core = self.member // 2, self.member % 2
        up, down, far = (ring + 1) % RING, (ring + RING - 1) % RING, (ring + 2) % RING
        self.up, self.down, self.far = up * 2 + core, down * 2 + core, far * 2 + core
        self.twin = ring * 2 + 1 - core
        self.twin_up, self.twin_down, self.twin_far = up * 2 + 1 - core, down * 2 + 1 - core, far * 2 + 1 - core

    def device(self, slot):
        return {"head": self.head, "frame": self.half * GROUP + slot}


def remote(src, dst, send, recv, device):
    copy = pltpu.make_async_remote_copy(
        src_ref=src, dst_ref=dst, send_sem=send, recv_sem=recv, device_id=device, device_id_type=MESH
    )
    copy.start()
    return copy


def arrived(part, sem):
    pltpu.make_async_copy(part, part, sem).wait()


def live_list(flags):
    spot = lax.broadcasted_iota(jnp.int32, (ENTRIES, ENTRIES), 0)
    later = lax.broadcasted_iota(jnp.int32, (ENTRIES, ENTRIES), 1)
    before = jnp.where(spot < later, 1.0, 0.0).astype(jnp.bfloat16)
    ahead = dot(flags.astype(jnp.bfloat16), before)
    lane = lax.broadcasted_iota(jnp.int32, (ROWS, ENTRIES), 1)
    value = lane.astype(jnp.float32) * flags
    ahead = jnp.where(flags > 0.0, ahead, -1.0)
    table = jnp.where(lane == COUNT_AT, jnp.sum(flags, axis=1, keepdims=True), 0.0)
    for k in range(SLOTS):
        found = jnp.sum(jnp.where(ahead == float(k), value, 0.0), axis=1, keepdims=True)
        table = jnp.where(lane == k, found, table)
    return table.astype(jnp.int32)


def write_tables(member, order_ref, live_ref, by_query_ref, by_key_ref):
    lane = lax.broadcasted_iota(jnp.int32, (1, ENTRIES), 1)
    order = jnp.zeros((1, ENTRIES), jnp.int32)
    for g in range(2 * GROUP):
        order = jnp.where(lane // NBLK == g, order_ref[g], order)
    rows = lax.broadcasted_iota(jnp.int32, (NBLK, ENTRIES), 0)
    lanes = lax.broadcasted_iota(jnp.int32, (NBLK, ENTRIES), 1)
    spread = jnp.where(lanes % NBLK == rows, 1.0, 0.0).astype(jnp.bfloat16)
    apart = lax.broadcasted_iota(jnp.int32, (NBLK, NBLK, 2 * GROUP), 2)
    query_rows, key_rows = [], []
    for unit in range(2):
        distance = jnp.abs(order - order_ref[unit * GROUP + member])
        by_query = jnp.zeros((NBLK, ENTRIES), jnp.float32)
        by_key = jnp.zeros((NBLK, ENTRIES), jnp.float32)
        for d in range(1, REACH):
            blocks = jnp.sum(jnp.where(apart == d, live_ref[...], 0), axis=2)
            blocks = blocks.astype(jnp.float32).astype(jnp.bfloat16)
            here = distance == d
            by_query = jnp.where(here, dot(blocks, spread), by_query)
            by_key = jnp.where(here, dot(blocks, spread, TN), by_key)
        query_rows.append(by_query)
        key_rows.append(by_key)
    by_query_ref[...] = live_list(jnp.concatenate(query_rows, axis=0))
    by_key_ref[...] = live_list(jnp.concatenate(key_rows, axis=0))


def gather_kernel(order_src, live_src, out_src, key_src, value_src, query_src, grad_src, key_all, value_all, query_all,
                  grad_all, delta_all, query_own, grad_own, peak, total, acc, by_query_ref, by_key_ref, grad_half, delta_src, raw,
                  grad_raw, out_raw, order_ref, live_ref, send1, recv1, send2, recv2, send3, recv3, load):
    ring = Ring()
    head, half, member = ring.head, ring.half, ring.member
    plane = head * 2 + half
    srcs = (key_src, value_src, query_src, grad_src, delta_src)
    bufs = (key_all, value_all, query_all, grad_all, delta_all)

    def plane_peer(step):
        other = (plane + step) % HEADS
        return other, {"head": other // 2, "frame": (other % 2) * GROUP + member}

    fetches = [
        pltpu.make_async_copy(grad_src, grad_raw, load.at[0]),
        pltpu.make_async_copy(out_src, out_raw, load.at[1]),
        pltpu.make_async_copy(order_src, order_ref, load.at[2]),
        pltpu.make_async_copy(live_src, live_ref, load.at[3]),
    ]
    for fetch in fetches:
        fetch.start()
    barrier = pltpu.get_barrier_semaphore()
    for step in range(1, HEADS):
        pl.semaphore_signal(barrier, inc=1, device_id=plane_peer(step)[1], device_id_type=MESH)
    for slot in (ring.up, ring.down, ring.twin):
        pl.semaphore_signal(barrier, inc=1, device_id=ring.device(slot), device_id_type=MESH)
    pl.semaphore_wait(barrier, HEADS - 1 + 3)

    pending = []
    pending.append(remote(query_src, raw.at[0], send3.at[0], recv3.at[0], ring.device(ring.up)))
    pending.append(remote(query_src, raw.at[1], send3.at[1], recv3.at[1], ring.device(ring.down)))

    def column(src, other):
        if src is delta_src:
            return src.at[other]
        return src.at[:, pl.ds(pl.multiple_of(other * HEAD_DIM, HEAD_DIM), HEAD_DIM)]

    def scatter(src, target, send, recv):
        for step in range(1, HEADS):
            other, device = plane_peer(step)
            remote(column(src, other), target, send, recv, device)
        pltpu.make_async_copy(column(src, plane), target, recv).start()

    for a in (KEY, VALUE, QUERY, GRAD):
        scatter(srcs[a], bufs[a].at[half, member, head], send1.at[a], recv1.at[a])
    fetches[0].wait()
    fetches[1].wait()
    for n in range(HEADS):
        lanes = slice(n * HEAD_DIM, (n + 1) * HEAD_DIM)
        products = grad_raw[:, lanes].astype(jnp.float32) * out_raw[:, lanes].astype(jnp.float32)
        delta_src[n] = jnp.sum(products.T, axis=0, keepdims=True)
    scatter(delta_src, bufs[DELTA].at[half, member, head], send1.at[DELTA], recv1.at[DELTA])

    def push(a, number, part, slot, arrive):
        pending.append(remote(part, part, send2.at[a, number], recv2.at[a, arrive], ring.device(slot)))

    def spread(a):
        own = bufs[a].at[:, member]
        arrived(own, recv1.at[a])
        if a != QUERY:
            near = bufs[a].at[0, member] if a == GRAD else own
            push(a, 0, near, ring.up, 0)
            push(a, 1, near, ring.down, 1)
        push(a, 2, own, ring.twin, 4)

    def pass_raw(number, slot):
        scatter(raw.at[number], bufs[QUERY].at[half, slot, head], send1.at[5 + number], recv1.at[5 + number])

    upper, lower = pl.ds(0, BLK // 2), pl.ds(BLK // 2, BLK // 2)
    spread(KEY)
    fetches[2].wait()
    fetches[3].wait()
    write_tables(member, order_ref, live_ref, by_query_ref, by_key_ref)
    spread(VALUE)
    arrived(raw.at[0], recv3.at[0])
    pending.append(remote(raw.at[0, upper], raw.at[2, upper], send3.at[2], recv3.at[2], ring.device(ring.up)))
    pass_raw(0, ring.down)
    arrived(raw.at[1], recv3.at[1])
    pending.append(remote(raw.at[1, lower], raw.at[2, lower], send3.at[3], recv3.at[3], ring.device(ring.down)))
    pass_raw(1, ring.up)
    spread(QUERY)
    fetch_query = pltpu.make_async_copy(bufs[QUERY].at[:, member], query_own, load.at[4])
    fetch_query.start()
    spread(GRAD)
    fetch_grad = pltpu.make_async_copy(bufs[GRAD].at[:, member], grad_own, load.at[5])
    fetch_grad.start()
    fetch_half = pltpu.make_async_copy(bufs[GRAD].at[1, member], grad_half, load.at[6])
    fetch_half.start()
    spread(DELTA)
    fetch_query.wait()
    fetch_grad.wait()
    fetch_half.wait()

    span = WIDE // BLK
    for unit in range(2):
        key = key_all[unit, member].reshape(NBLK * BLK, HEAD_DIM)
        value = value_all[unit, member].reshape(NBLK * BLK, HEAD_DIM)
        for i in range(0, NBLK, span):
            query = query_own[unit, i : i + span].reshape(WIDE, HEAD_DIM)
            grad = grad_own[unit, i : i + span].reshape(WIDE, HEAD_DIM)
            delta = jnp.concatenate([delta_all[unit, member, i + s] for s in range(span)], axis=1)
            scores = dot(key, query, NT) * SCALE2
            top = jnp.max(scores, axis=0, keepdims=True)
            probs = jnp.exp2(scores - top)
            summed = jnp.sum(probs, axis=0, keepdims=True)
            grads = dot(value, grad, NT) - delta
            partial = dot(key, (probs * grads).astype(jnp.bfloat16), TN)
            for s in range(span):
                lanes = slice(s * BLK, (s + 1) * BLK)
                row = unit * NBLK + i + s
                peak[row] = top[:, lanes]
                total[row] = summed[:, lanes]
                acc[row] = partial[:, lanes]

    arrived(raw.at[2, upper], recv3.at[2])
    arrived(raw.at[2, lower], recv3.at[3])
    pass_raw(2, ring.far)
    arrived(bufs[QUERY].at[:, ring.down], recv1.at[5])
    push(QUERY, 4, bufs[QUERY].at[:, ring.down], ring.twin, 5)
    arrived(bufs[QUERY].at[:, ring.up], recv1.at[6])
    push(QUERY, 6, bufs[QUERY].at[:, ring.up], ring.twin, 6)
    for a in (KEY, VALUE, GRAD, DELTA):
        part = bufs[a].at[0, ring.down] if a == GRAD else bufs[a].at[:, ring.down]
        arrived(part, recv2.at[a, 0])
        if a != GRAD:
            push(a, 3, bufs[a].at[0, ring.down], ring.up, 2)
        push(a, 4, part, ring.twin, 5)
        part = bufs[a].at[0, ring.up] if a == GRAD else bufs[a].at[:, ring.up]
        arrived(part, recv2.at[a, 1])
        if a != GRAD:
            push(a, 5, bufs[a].at[1, ring.up], ring.down, 3)
        push(a, 6, part, ring.twin, 6)
    arrived(bufs[QUERY].at[:, ring.far], recv1.at[7])
    push(QUERY, 7, bufs[QUERY].at[:, ring.far], ring.twin, 7)
    for a in (KEY, VALUE, DELTA):
        part = bufs[a].at[0, ring.far]
        arrived(part, recv2.at[a, 2])
        push(a, 7, part, ring.twin, 7)
        part = bufs[a].at[1, ring.far]
        arrived(part, recv2.at[a, 3])
        push(a, 8, part, ring.twin, 8)
    for a in (KEY, VALUE, QUERY, GRAD, DELTA):
        arrived(bufs[a].at[:, ring.twin], recv2.at[a, 4])
        for number, slot in ((5, ring.twin_down), (6, ring.twin_up)):
            arrived(bufs[a].at[0, slot] if a == GRAD else bufs[a].at[:, slot], recv2.at[a, number])
        if a == QUERY:
            arrived(bufs[a].at[:, ring.twin_far], recv2.at[a, 7])
        elif a != GRAD:
            arrived(bufs[a].at[0, ring.twin_far], recv2.at[a, 7])
            arrived(bufs[a].at[1, ring.twin_far], recv2.at[a, 8])
    for copy in pending:
        copy.wait_send()
    for a in range(8):
        source = srcs[a] if a < 5 else raw.at[a - 5]
        sent = source.at[pl.ds(0, HEADS - 1)] if a == DELTA else source.at[:, pl.ds(0, (HEADS - 1) * HEAD_DIM)]
        arrived(sent, send1.at[a])


WHOLE = (2, GROUP, NBLK, BLK, HEAD_DIM)
STATS = (2, GROUP, NBLK, 1, BLK)
OWN = (2, NBLK, BLK, HEAD_DIM)
LIMIT = 20 << 20


def gather_all(order, live, key, value, query, grad, out):
    low, full, whole = jnp.bfloat16, jnp.float32, jnp.int32
    return pl.pallas_call(
        gather_kernel,
        out_shape=(
            jax.ShapeDtypeStruct(WHOLE, low),
            jax.ShapeDtypeStruct(WHOLE, low),
            jax.ShapeDtypeStruct(WHOLE, low),
            jax.ShapeDtypeStruct(WHOLE, low),
            jax.ShapeDtypeStruct(STATS, full),
            jax.ShapeDtypeStruct(OWN, low),
            jax.ShapeDtypeStruct(OWN, low),
            jax.ShapeDtypeStruct((ROWS, 1, BLK), full),
            jax.ShapeDtypeStruct((ROWS, 1, BLK), full),
            jax.ShapeDtypeStruct((ROWS, HEAD_DIM, BLK), full),
            jax.ShapeDtypeStruct((ROWS, ENTRIES), whole),
            jax.ShapeDtypeStruct((ROWS, ENTRIES), whole),
            jax.ShapeDtypeStruct(OWN[1:], low),
        ),
        in_specs=[HBM] * 7,
        out_specs=(VMEM, VMEM, VMEM, ANY) + (VMEM,) * 9,
        scratch_shapes=[
            pltpu.VMEM((HEADS, 1, BLK), full),
            pltpu.VMEM((3, BLK, HEADS * HEAD_DIM), low),
            pltpu.VMEM((BLK, HEADS * HEAD_DIM), low),
            pltpu.VMEM((BLK, HEADS * HEAD_DIM), low),
            pltpu.SMEM((2 * GROUP,), whole),
            pltpu.VMEM((NBLK, NBLK, 2 * GROUP), whole),
            pltpu.SemaphoreType.DMA((8,)),
            pltpu.SemaphoreType.DMA((8,)),
            pltpu.SemaphoreType.DMA((5, 9)),
            pltpu.SemaphoreType.DMA((5, 9)),
            pltpu.SemaphoreType.DMA((4,)),
            pltpu.SemaphoreType.DMA((4,)),
            pltpu.SemaphoreType.DMA((7,)),
        ],
        compiler_params=pltpu.CompilerParams(collective_id=0, has_side_effects=True, vmem_limit_bytes=LIMIT),
        name="gather_all",
    )(*(pltpu.with_memory_space_constraint(x, pltpu.HBM) for x in (order, live, out, key, value, query, grad)))


def turns(table, rows):
    most = table[rows[0], COUNT_AT]
    for row in rows[1:]:
        most = jnp.maximum(most, table[row, COUNT_AT])
    return (most + CHUNK - 1) // CHUNK


def query_kernel(table, query_own, grad_own, delta_all, key_ref, value_ref, peak_in, total_in, acc_in, kept_ref, sent_ref, lse_ref,
                 peak, total, acc):
    member = place()[2]
    peak[...] = peak_in[...]
    total[...] = total_in[...]
    acc[...] = acc_in[...]

    def step(turn, carry):
        for first in range(0, ROWS, PAIR):
            rows = range(first, first + PAIR)
            keys, scores, grads = [], [], []
            for row in rows:
                unit, i = row // NBLK, row % NBLK
                slots = [turn * CHUNK + c for c in range(CHUNK)]
                entries = [table[row, slot] for slot in slots]
                bias = [jnp.where(slot < table[row, COUNT_AT], 0.0, -FAR) for slot in slots]
                key = jnp.concatenate([key_ref[e] for e in entries], axis=0)
                value = jnp.concatenate([value_ref[e] for e in entries], axis=0)
                s = dot(key, query_own[unit, i], NT)
                s = jnp.concatenate([s[c * BLK : (c + 1) * BLK] * SCALE2 + bias[c] for c in range(CHUNK)], axis=0)
                keys.append(key)
                scores.append(s)
                grads.append(dot(value, grad_own[unit, i], NT) - delta_all[unit, member, i])
            results = []
            for n, row in enumerate(rows):
                before = peak[row]
                top = jnp.maximum(before, jnp.max(scores[n], axis=0, keepdims=True))
                probs = jnp.exp2(scores[n] - top)
                terms = (probs * grads[n]).astype(jnp.bfloat16)
                results.append((top, jnp.exp2(before - top), jnp.sum(probs, axis=0, keepdims=True), dot(keys[n], terms, TN)))
            for n, row in enumerate(rows):
                top, shrink, summed, product = results[n]
                peak[row] = top
                total[row] = total[row] * shrink + summed
                acc[row] = acc[row] * shrink + product
        return carry

    lax.fori_loop(0, turns(table, range(ROWS)), step, 0)
    first = place()[1] == 0
    for i in range(NBLK):
        done = []
        for unit in range(2):
            row = unit * NBLK + i
            lse_ref[unit, i] = peak[row] + jnp.log2(total[row])
            done.append((acc[row] * (SCALE / total[row])).T.astype(jnp.bfloat16))
        kept_ref[i] = jnp.where(first, done[0], done[1])
        sent_ref[i] = jnp.where(first, done[1], done[0])


def flat(array):
    return array.reshape((ENTRIES,) + array.shape[3:])


def query_pass(table, query_own, grad_own, delta, key, value, peak, total, acc):
    return pl.pallas_call(
        query_kernel,
        out_shape=(
            jax.ShapeDtypeStruct(OWN[1:], jnp.bfloat16),
            jax.ShapeDtypeStruct(OWN[1:], jnp.bfloat16),
            jax.ShapeDtypeStruct((2, NBLK, 1, BLK), jnp.float32),
        ),
        in_specs=[SMEM] + [VMEM] * 8,
        out_specs=(VMEM,) * 3,
        scratch_shapes=[
            pltpu.VMEM((ROWS, 1, BLK), jnp.float32),
            pltpu.VMEM((ROWS, 1, BLK), jnp.float32),
            pltpu.VMEM((ROWS, HEAD_DIM, BLK), jnp.float32),
        ],
        compiler_params=pltpu.CompilerParams(vmem_limit_bytes=LIMIT),
        cost_estimate=pl.CostEstimate(flops=4_000_000_000, bytes_accessed=8 << 20, transcendentals=1 << 21),
        name="query_pass",
    )(table, query_own, grad_own, delta, flat(key), flat(value), peak, total, acc)


def diagonal(unit, member, query_own, grad_own, key_all, value_all, delta_at, lse_at, key_acc, value_acc):
    query = query_own[unit].reshape(NBLK * BLK, HEAD_DIM)
    grad = grad_own[unit].reshape(NBLK * BLK, HEAD_DIM)
    delta = jnp.concatenate([delta_at(unit, i) for i in range(NBLK)], axis=1)
    lse = jnp.concatenate([lse_at(unit, i) for i in range(NBLK)], axis=1)
    span = WIDE // BLK
    for u in range(0, NBLK, span):
        key = key_all[unit, member, u : u + span].reshape(WIDE, HEAD_DIM)
        value = value_all[unit, member, u : u + span].reshape(WIDE, HEAD_DIM)
        probs = jnp.exp2(dot(key, query, NT) * SCALE2 - lse)
        terms = (probs * (dot(value, grad, NT) - delta)).astype(jnp.bfloat16)
        value_part = dot(probs.astype(jnp.bfloat16), grad)
        key_part = dot(terms, query)
        for s in range(span):
            rows = slice(s * BLK, (s + 1) * BLK)
            value_acc[u + s] = value_part[rows]
            key_acc[u + s] = key_part[rows]


def share_kernel(lse_own, delta_all, query_own, grad_own, key_all, value_all, from_down, from_up, grad_part, lse_all, grad_all,
                 key_acc, value_acc, send, recv, send2, recv2, load):
    ring = Ring()
    member = ring.member

    barrier = pltpu.get_barrier_semaphore()
    for step in range(1, GROUP):
        slot = (member + step) % GROUP
        pl.semaphore_signal(barrier, inc=1, device_id=ring.device(slot), device_id_type=MESH)
    pl.semaphore_wait(barrier, GROUP - 1)
    pending = []
    for step in range(1, GROUP):
        device = ring.device((member + step) % GROUP)
        pending.append(remote(lse_own, lse_all.at[:, member], send.at[step], recv.at[step], device))

    def push(number, part, target, slot):
        pending.append(remote(part, target, send2.at[number], recv2.at[number], ring.device(slot)))

    push(0, grad_part.at[0, ring.down], grad_all.at[0, ring.down], ring.up)
    push(1, from_up, grad_all.at[1, ring.up], ring.down)
    push(2, from_down, grad_all.at[1, ring.down], ring.twin)
    push(3, from_up, grad_all.at[1, ring.up], ring.twin)
    held = [(lse_own, lse_all.at[:, member]), (from_down, grad_all.at[1, ring.down]), (from_up, grad_all.at[1, ring.up])]
    for slot in (ring.member, ring.twin):
        held.append((grad_part.at[:, slot], grad_all.at[:, slot]))
    for slot in (ring.down, ring.up, ring.twin_down, ring.twin_up):
        held.append((grad_part.at[0, slot], grad_all.at[0, slot]))
    loads = [pltpu.make_async_copy(part, target, load.at[n]) for n, (part, target) in enumerate(held)]
    for copy in loads:
        copy.start()

    diagonal(1 - ring.half, member, query_own, grad_own, key_all, value_all,
             lambda unit, i: delta_all[unit, member, i], lambda unit, i: lse_own[unit, i], key_acc, value_acc)

    far = (grad_all.at[0, ring.far], grad_all.at[1, ring.far])
    for n in range(2):
        arrived(far[n], recv2.at[n])
        push(4 + n, far[n], far[n], ring.twin)
    for copy in loads:
        copy.wait()
    for step in range(1, GROUP):
        arrived(lse_own, recv.at[step])
    arrived(grad_all.at[1, ring.twin_down], recv2.at[2])
    arrived(grad_all.at[1, ring.twin_up], recv2.at[3])
    arrived(grad_all.at[0, ring.twin_far], recv2.at[4])
    arrived(grad_all.at[1, ring.twin_far], recv2.at[5])
    for copy in pending:
        copy.wait_send()


def share_totals(lse_own, delta, query_own, grad_own, key, value, from_down, from_up, grad):
    return pl.pallas_call(
        share_kernel,
        out_shape=(
            jax.ShapeDtypeStruct(STATS, jnp.float32),
            jax.ShapeDtypeStruct(WHOLE, jnp.bfloat16),
            jax.ShapeDtypeStruct((NBLK, BLK, HEAD_DIM), jnp.float32),
            jax.ShapeDtypeStruct((NBLK, BLK, HEAD_DIM), jnp.float32),
        ),
        in_specs=[VMEM] * 8 + [ANY],
        out_specs=(VMEM,) * 4,
        scratch_shapes=[
            pltpu.SemaphoreType.DMA((GROUP,)),
            pltpu.SemaphoreType.DMA((GROUP,)),
            pltpu.SemaphoreType.DMA((6,)),
            pltpu.SemaphoreType.DMA((6,)),
            pltpu.SemaphoreType.DMA((9,)),
        ],
        compiler_params=pltpu.CompilerParams(collective_id=1, has_side_effects=True, vmem_limit_bytes=LIMIT),
        name="share_totals",
    )(lse_own, delta, query_own, grad_own, key, value, from_down, from_up, grad)


def key_kernel(blocks, table, key_all, value_all, delta_ref, lse_ref, query_ref, grad_ref, first_in, second_in, out_ref,
               key_acc, value_acc):
    _, half, member = place()
    other = len(blocks) < NBLK
    unit = 1 - half if other else half
    base = unit * NBLK
    if other:
        for u in blocks:
            key_acc[u] = first_in[u]
            value_acc[u] = second_in[u]
    else:
        own = (unit * GROUP + member) * NBLK
        diagonal(unit, member, first_in, second_in, key_all, value_all,
                 lambda unit, i: delta_ref[own + i], lambda unit, i: lse_ref[own + i], key_acc, value_acc)

    def step(turn, carry):
        for first in blocks[::PAIR]:
            pair = range(first, first + PAIR)
            loads, results = [], []
            for u in pair:
                row = base + u
                slots = [turn * CHUNK + c for c in range(CHUNK)]
                entries = [table[row, slot] for slot in slots]
                bias = [jnp.where(slot < table[row, COUNT_AT], 0.0, FAR) for slot in slots]
                query = jnp.concatenate([query_ref[e] for e in entries], axis=0)
                grad = jnp.concatenate([grad_ref[e] for e in entries], axis=0)
                lse = jnp.concatenate([lse_ref[e] + b for e, b in zip(entries, bias)], axis=1)
                delta = jnp.concatenate([delta_ref[e] for e in entries], axis=1)
                scores = dot(key_all[unit, member, u], query, NT)
                grads = dot(value_all[unit, member, u], grad, NT)
                loads.append((query, grad, lse, delta, scores, grads))
            for query, grad, lse, delta, scores, grads in loads:
                probs = jnp.exp2(scores * SCALE2 - lse)
                terms = (probs * (grads - delta)).astype(jnp.bfloat16)
                results.append((dot(probs.astype(jnp.bfloat16), grad), dot(terms, query)))
            for n, u in enumerate(pair):
                value_acc[u] += results[n][0]
                key_acc[u] += results[n][1]
        return carry

    lax.fori_loop(0, turns(table, [base + u for u in blocks]), step, 0)
    for n, u in enumerate(blocks):
        out_ref[0, n] = (key_acc[u] * SCALE).astype(jnp.bfloat16)
        out_ref[1, n] = value_acc[u].astype(jnp.bfloat16)


def key_pass(blocks, table, key, value, delta, lse, query, grad, first, second):
    def kernel(*refs):
        key_kernel(blocks, *refs)

    return pl.pallas_call(
        kernel,
        out_shape=jax.ShapeDtypeStruct((2, len(blocks), BLK, HEAD_DIM), jnp.bfloat16),
        in_specs=[SMEM] + [VMEM] * 8,
        out_specs=VMEM,
        scratch_shapes=[
            pltpu.VMEM((NBLK, BLK, HEAD_DIM), jnp.float32),
            pltpu.VMEM((NBLK, BLK, HEAD_DIM), jnp.float32),
        ],
        compiler_params=pltpu.CompilerParams(vmem_limit_bytes=LIMIT),
        cost_estimate=pl.CostEstimate(flops=2_000_000_000, bytes_accessed=1 << 20, transcendentals=1 << 20),
        name="key_pass",
    )(table, key, value, flat(delta), flat(lse), flat(query), flat(grad), first, second)


def local(queries, key_states, value_states, attn_out, grad_out, frame_order, block_live):
    first = lax.axis_index("frame") < GROUP
    frame_order, first = lax.optimization_barrier((frame_order, first))
    (key, value, query, grad, delta, query_own, grad_own, peak, total, acc, by_query, by_key, grad_half) = gather_all(
        frame_order, block_live.transpose(1, 2, 0), key_states, value_states, queries, grad_out, attn_out
    )
    round_up = [(source, source // GROUP * GROUP + (source + 2) % GROUP) for source in range(2 * GROUP)]
    from_down = lax.ppermute(grad_half, "frame", round_up)
    from_up = lax.ppermute(grad_half, "frame", [(target, source) for source, target in round_up])
    dq_kept, dq_sent, lse_own = query_pass(by_query, query_own, grad_own, delta, key, value, peak, total, acc)
    swap = [(source, (source + GROUP) % (2 * GROUP)) for source in range(2 * GROUP)]

    def across(sent):
        return lax.ppermute(sent, "frame", swap)

    def join(kept, came):
        kept, came = kept.reshape(NBLK * BLK, HEAD_DIM), came.reshape(NBLK * BLK, HEAD_DIM)
        return jnp.concatenate([jnp.where(first, kept, came), jnp.where(first, came, kept)], axis=1)

    dq_came = across(dq_sent)
    lse, grad, key_acc, value_acc = share_totals(
        lse_own, delta, query_own, grad_own, key, value, from_down, from_up, grad
    )
    gathered = (by_key, key, value, delta, lse, query, grad)
    middle = NBLK // 2
    came = [
        across(key_pass(blocks, *gathered, key_acc, value_acc)) for blocks in (range(middle), range(middle, NBLK))
    ]
    came = jnp.concatenate(came, axis=1)
    kept = key_pass(range(NBLK), *gathered, query_own, grad_own)
    return join(dq_kept, dq_came), join(kept[0], came[0]), join(kept[1], came[1])


def solution(mesh):
    rows = P(("frame", "head"), None)
    out = P("frame", "head")
    return jax.shard_map(
        local,
        mesh=mesh,
        in_specs=(rows, rows, rows, rows, rows, P(), P()),
        out_specs=(out, out, out),
        check_vma=False,
    )
```

```python
import math

import jax
import jax.numpy as jnp
from jax import lax
from jax.experimental import pallas as pl
from jax.experimental.pallas import tpu as pltpu
from jax.sharding import PartitionSpec as P

HEADS = 16
HEAD_DIM = 128
SCALE = HEAD_DIM ** (-0.5)
SCALE2 = SCALE * math.log2(math.e)
REACH = 4
NBLK = 8
BLK = 128
RING = 4
GROUP = 8
ROWS = 2 * NBLK
ENTRIES = 2 * GROUP * NBLK
SLOTS = 2 * (REACH - 1) * NBLK
COUNT_AT = BLK - 1
CHUNK = 5
PAIR = 4
WIDE = 512
FAR = 1e30
MESH = pl.DeviceIdType.MESH
ANY = pl.BlockSpec(memory_space=pl.ANY)
SMEM = pl.BlockSpec(memory_space=pltpu.SMEM)
HBM = pl.BlockSpec(memory_space=pltpu.HBM)
VMEM = pl.BlockSpec(memory_space=pltpu.VMEM)
NN = (((1,), (0,)), ((), ()))
NT = (((1,), (1,)), ((), ()))
TN = (((0,), (0,)), ((), ()))
KEY, VALUE, QUERY, GRAD, DELTA = range(5)


def dot(a, b, dims=NN):
    return lax.dot_general(a, b, dims, preferred_element_type=jnp.float32)


def place():
    frame = lax.axis_index("frame")
    return lax.axis_index("head"), frame // GROUP, frame % GROUP


class Ring:
    def __init__(self):
        self.head, self.half, self.member = place()
        ring, core = self.member // 2, self.member % 2
        up, down, far = (ring + 1) % RING, (ring + RING - 1) % RING, (ring + 2) % RING
        self.up, self.down, self.far = up * 2 + core, down * 2 + core, far * 2 + core
        self.twin = ring * 2 + 1 - core
        self.twin_up, self.twin_down, self.twin_far = up * 2 + 1 - core, down * 2 + 1 - core, far * 2 + 1 - core

    def device(self, slot):
        return {"head": self.head, "frame": self.half * GROUP + slot}


def remote(src, dst, send, recv, device):
    copy = pltpu.make_async_remote_copy(
        src_ref=src, dst_ref=dst, send_sem=send, recv_sem=recv, device_id=device, device_id_type=MESH
    )
    copy.start()
    return copy


def arrived(part, sem):
    pltpu.make_async_copy(part, part, sem).wait()


def live_list(flags):
    spot = lax.broadcasted_iota(jnp.int32, (ENTRIES, ENTRIES), 0)
    later = lax.broadcasted_iota(jnp.int32, (ENTRIES, ENTRIES), 1)
    before = jnp.where(spot < later, 1.0, 0.0).astype(jnp.bfloat16)
    ahead = dot(flags.astype(jnp.bfloat16), before)
    lane = lax.broadcasted_iota(jnp.int32, (ROWS, ENTRIES), 1)
    value = lane.astype(jnp.float32) * flags
    ahead = jnp.where(flags > 0.0, ahead, -1.0)
    table = jnp.where(lane == COUNT_AT, jnp.sum(flags, axis=1, keepdims=True), 0.0)
    for k in range(SLOTS):
        found = jnp.sum(jnp.where(ahead == float(k), value, 0.0), axis=1, keepdims=True)
        table = jnp.where(lane == k, found, table)
    return table.astype(jnp.int32)


def write_tables(member, order_ref, live_ref, by_query_ref, by_key_ref):
    lane = lax.broadcasted_iota(jnp.int32, (1, ENTRIES), 1)
    order = jnp.zeros((1, ENTRIES), jnp.int32)
    for g in range(2 * GROUP):
        order = jnp.where(lane // NBLK == g, order_ref[g], order)
    rows = lax.broadcasted_iota(jnp.int32, (NBLK, ENTRIES), 0)
    lanes = lax.broadcasted_iota(jnp.int32, (NBLK, ENTRIES), 1)
    spread = jnp.where(lanes % NBLK == rows, 1.0, 0.0).astype(jnp.bfloat16)
    apart = lax.broadcasted_iota(jnp.int32, (NBLK, NBLK, 2 * GROUP), 2)
    query_rows, key_rows = [], []
    for unit in range(2):
        distance = jnp.abs(order - order_ref[unit * GROUP + member])
        by_query = jnp.zeros((NBLK, ENTRIES), jnp.float32)
        by_key = jnp.zeros((NBLK, ENTRIES), jnp.float32)
        for d in range(1, REACH):
            blocks = jnp.sum(jnp.where(apart == d, live_ref[...], 0), axis=2)
            blocks = blocks.astype(jnp.float32).astype(jnp.bfloat16)
            here = distance == d
            by_query = jnp.where(here, dot(blocks, spread), by_query)
            by_key = jnp.where(here, dot(blocks, spread, TN), by_key)
        query_rows.append(by_query)
        key_rows.append(by_key)
    by_query_ref[...] = live_list(jnp.concatenate(query_rows, axis=0))
    by_key_ref[...] = live_list(jnp.concatenate(key_rows, axis=0))


def gather_kernel(order_src, live_src, out_src, key_src, value_src, query_src, grad_src, key_all, value_all, query_all,
                  grad_all, delta_all, query_own, grad_own, peak, total, acc, by_query_ref, by_key_ref, grad_half, delta_src, raw,
                  grad_raw, out_raw, order_ref, live_ref, send1, recv1, send2, recv2, send3, recv3, load):
    ring = Ring()
    head, half, member = ring.head, ring.half, ring.member
    plane = head * 2 + half
    srcs = (key_src, value_src, query_src, grad_src, delta_src)
    bufs = (key_all, value_all, query_all, grad_all, delta_all)

    def plane_peer(step):
        other = (plane + step) % HEADS
        return other, {"head": other // 2, "frame": (other % 2) * GROUP + member}

    fetches = [
        pltpu.make_async_copy(grad_src, grad_raw, load.at[0]),
        pltpu.make_async_copy(out_src, out_raw, load.at[1]),
        pltpu.make_async_copy(order_src, order_ref, load.at[2]),
        pltpu.make_async_copy(live_src, live_ref, load.at[3]),
    ]
    for fetch in fetches:
        fetch.start()
    barrier = pltpu.get_barrier_semaphore()
    for step in range(1, HEADS):
        pl.semaphore_signal(barrier, inc=1, device_id=plane_peer(step)[1], device_id_type=MESH)
    for slot in (ring.up, ring.down, ring.twin):
        pl.semaphore_signal(barrier, inc=1, device_id=ring.device(slot), device_id_type=MESH)
    pl.semaphore_wait(barrier, HEADS - 1 + 3)

    pending = []
    pending.append(remote(query_src, raw.at[0], send3.at[0], recv3.at[0], ring.device(ring.up)))
    pending.append(remote(query_src, raw.at[1], send3.at[1], recv3.at[1], ring.device(ring.down)))

    def column(src, other):
        if src is delta_src:
            return src.at[other]
        return src.at[:, pl.ds(pl.multiple_of(other * HEAD_DIM, HEAD_DIM), HEAD_DIM)]

    def scatter(src, target, send, recv):
        for step in range(1, HEADS):
            other, device = plane_peer(step)
            remote(column(src, other), target, send, recv, device)
        pltpu.make_async_copy(column(src, plane), target, recv).start()

    for a in (KEY, VALUE, QUERY, GRAD):
        scatter(srcs[a], bufs[a].at[half, member, head], send1.at[a], recv1.at[a])
    fetches[0].wait()
    fetches[1].wait()
    for n in range(HEADS):
        lanes = slice(n * HEAD_DIM, (n + 1) * HEAD_DIM)
        products = grad_raw[:, lanes].astype(jnp.float32) * out_raw[:, lanes].astype(jnp.float32)
        delta_src[n] = jnp.sum(products.T, axis=0, keepdims=True)
    scatter(delta_src, bufs[DELTA].at[half, member, head], send1.at[DELTA], recv1.at[DELTA])

    def push(a, number, part, slot, arrive):
        pending.append(remote(part, part, send2.at[a, number], recv2.at[a, arrive], ring.device(slot)))

    def spread(a):
        own = bufs[a].at[:, member]
        arrived(own, recv1.at[a])
        if a != QUERY:
            near = bufs[a].at[0, member] if a == GRAD else own
            push(a, 0, near, ring.up, 0)
            push(a, 1, near, ring.down, 1)
        push(a, 2, own, ring.twin, 4)

    def pass_raw(number, slot):
        scatter(raw.at[number], bufs[QUERY].at[half, slot, head], send1.at[5 + number], recv1.at[5 + number])

    upper, lower = pl.ds(0, BLK // 2), pl.ds(BLK // 2, BLK // 2)
    spread(KEY)
    fetches[2].wait()
    fetches[3].wait()
    write_tables(member, order_ref, live_ref, by_query_ref, by_key_ref)
    spread(VALUE)
    arrived(raw.at[0], recv3.at[0])
    pending.append(remote(raw.at[0, upper], raw.at[2, upper], send3.at[2], recv3.at[2], ring.device(ring.up)))
    pass_raw(0, ring.down)
    arrived(raw.at[1], recv3.at[1])
    pending.append(remote(raw.at[1, lower], raw.at[2, lower], send3.at[3], recv3.at[3], ring.device(ring.down)))
    pass_raw(1, ring.up)
    spread(QUERY)
    fetch_query = pltpu.make_async_copy(bufs[QUERY].at[:, member], query_own, load.at[4])
    fetch_query.start()
    spread(GRAD)
    fetch_grad = pltpu.make_async_copy(bufs[GRAD].at[:, member], grad_own, load.at[5])
    fetch_grad.start()
    fetch_half = pltpu.make_async_copy(bufs[GRAD].at[1, member], grad_half, load.at[6])
    fetch_half.start()
    spread(DELTA)
    fetch_query.wait()
    fetch_grad.wait()
    fetch_half.wait()

    span = WIDE // BLK
    for unit in range(2):
        key = key_all[unit, member].reshape(NBLK * BLK, HEAD_DIM)
        value = value_all[unit, member].reshape(NBLK * BLK, HEAD_DIM)
        for i in range(0, NBLK, span):
            query = query_own[unit, i : i + span].reshape(WIDE, HEAD_DIM)
            grad = grad_own[unit, i : i + span].reshape(WIDE, HEAD_DIM)
            delta = jnp.concatenate([delta_all[unit, member, i + s] for s in range(span)], axis=1)
            scores = dot(key, query, NT) * SCALE2
            top = jnp.max(scores, axis=0, keepdims=True)
            probs = jnp.exp2(scores - top)
            summed = jnp.sum(probs, axis=0, keepdims=True)
            grads = dot(value, grad, NT) - delta
            partial = dot(key, (probs * grads).astype(jnp.bfloat16), TN)
            for s in range(span):
                lanes = slice(s * BLK, (s + 1) * BLK)
                row = unit * NBLK + i + s
                peak[row] = top[:, lanes]
                total[row] = summed[:, lanes]
                acc[row] = partial[:, lanes]

    arrived(raw.at[2, upper], recv3.at[2])
    arrived(raw.at[2, lower], recv3.at[3])
    pass_raw(2, ring.far)
    arrived(bufs[QUERY].at[:, ring.down], recv1.at[5])
    push(QUERY, 4, bufs[QUERY].at[:, ring.down], ring.twin, 5)
    arrived(bufs[QUERY].at[:, ring.up], recv1.at[6])
    push(QUERY, 6, bufs[QUERY].at[:, ring.up], ring.twin, 6)
    for a in (KEY, VALUE, GRAD, DELTA):
        part = bufs[a].at[0, ring.down] if a == GRAD else bufs[a].at[:, ring.down]
        arrived(part, recv2.at[a, 0])
        if a != GRAD:
            push(a, 3, bufs[a].at[0, ring.down], ring.up, 2)
        push(a, 4, part, ring.twin, 5)
        part = bufs[a].at[0, ring.up] if a == GRAD else bufs[a].at[:, ring.up]
        arrived(part, recv2.at[a, 1])
        if a != GRAD:
            push(a, 5, bufs[a].at[1, ring.up], ring.down, 3)
        push(a, 6, part, ring.twin, 6)
    arrived(bufs[QUERY].at[:, ring.far], recv1.at[7])
    push(QUERY, 7, bufs[QUERY].at[:, ring.far], ring.twin, 7)
    for a in (KEY, VALUE, DELTA):
        part = bufs[a].at[0, ring.far]
        arrived(part, recv2.at[a, 2])
        push(a, 7, part, ring.twin, 7)
        part = bufs[a].at[1, ring.far]
        arrived(part, recv2.at[a, 3])
        push(a, 8, part, ring.twin, 8)
    for a in (KEY, VALUE, QUERY, GRAD, DELTA):
        arrived(bufs[a].at[:, ring.twin], recv2.at[a, 4])
        for number, slot in ((5, ring.twin_down), (6, ring.twin_up)):
            arrived(bufs[a].at[0, slot] if a == GRAD else bufs[a].at[:, slot], recv2.at[a, number])
        if a == QUERY:
            arrived(bufs[a].at[:, ring.twin_far], recv2.at[a, 7])
        elif a != GRAD:
            arrived(bufs[a].at[0, ring.twin_far], recv2.at[a, 7])
            arrived(bufs[a].at[1, ring.twin_far], recv2.at[a, 8])
    for copy in pending:
        copy.wait_send()
    for a in range(8):
        source = srcs[a] if a < 5 else raw.at[a - 5]
        sent = source.at[pl.ds(0, HEADS - 1)] if a == DELTA else source.at[:, pl.ds(0, (HEADS - 1) * HEAD_DIM)]
        arrived(sent, send1.at[a])


WHOLE = (2, GROUP, NBLK, BLK, HEAD_DIM)
STATS = (2, GROUP, NBLK, 1, BLK)
OWN = (2, NBLK, BLK, HEAD_DIM)
LIMIT = 20 << 20


def gather_all(order, live, key, value, query, grad, out):
    low, full, whole = jnp.bfloat16, jnp.float32, jnp.int32
    return pl.pallas_call(
        gather_kernel,
        out_shape=(
            jax.ShapeDtypeStruct(WHOLE, low),
            jax.ShapeDtypeStruct(WHOLE, low),
            jax.ShapeDtypeStruct(WHOLE, low),
            jax.ShapeDtypeStruct(WHOLE, low),
            jax.ShapeDtypeStruct(STATS, full),
            jax.ShapeDtypeStruct(OWN, low),
            jax.ShapeDtypeStruct(OWN, low),
            jax.ShapeDtypeStruct((ROWS, 1, BLK), full),
            jax.ShapeDtypeStruct((ROWS, 1, BLK), full),
            jax.ShapeDtypeStruct((ROWS, HEAD_DIM, BLK), full),
            jax.ShapeDtypeStruct((ROWS, ENTRIES), whole),
            jax.ShapeDtypeStruct((ROWS, ENTRIES), whole),
            jax.ShapeDtypeStruct(OWN[1:], low),
        ),
        in_specs=[HBM] * 7,
        out_specs=(VMEM, VMEM, VMEM, ANY) + (VMEM,) * 9,
        scratch_shapes=[
            pltpu.VMEM((HEADS, 1, BLK), full),
            pltpu.VMEM((3, BLK, HEADS * HEAD_DIM), low),
            pltpu.VMEM((BLK, HEADS * HEAD_DIM), low),
            pltpu.VMEM((BLK, HEADS * HEAD_DIM), low),
            pltpu.SMEM((2 * GROUP,), whole),
            pltpu.VMEM((NBLK, NBLK, 2 * GROUP), whole),
            pltpu.SemaphoreType.DMA((8,)),
            pltpu.SemaphoreType.DMA((8,)),
            pltpu.SemaphoreType.DMA((5, 9)),
            pltpu.SemaphoreType.DMA((5, 9)),
            pltpu.SemaphoreType.DMA((4,)),
            pltpu.SemaphoreType.DMA((4,)),
            pltpu.SemaphoreType.DMA((7,)),
        ],
        compiler_params=pltpu.CompilerParams(collective_id=0, has_side_effects=True, vmem_limit_bytes=LIMIT),
        name="gather_all",
    )(*(pltpu.with_memory_space_constraint(x, pltpu.HBM) for x in (order, live, out, key, value, query, grad)))


def turns(table, rows):
    most = table[rows[0], COUNT_AT]
    for row in rows[1:]:
        most = jnp.maximum(most, table[row, COUNT_AT])
    return (most + CHUNK - 1) // CHUNK


def query_kernel(table, query_own, grad_own, delta_all, key_ref, value_ref, peak_in, total_in, acc_in, kept_ref, sent_ref, lse_ref,
                 peak, total, acc):
    member = place()[2]
    peak[...] = peak_in[...]
    total[...] = total_in[...]
    acc[...] = acc_in[...]

    def step(turn, carry):
        for first in range(0, ROWS, PAIR):
            rows = range(first, first + PAIR)
            keys, scores, grads = [], [], []
            for row in rows:
                unit, i = row // NBLK, row % NBLK
                slots = [turn * CHUNK + c for c in range(CHUNK)]
                entries = [table[row, slot] for slot in slots]
                bias = [jnp.where(slot < table[row, COUNT_AT], 0.0, -FAR) for slot in slots]
                key = jnp.concatenate([key_ref[e] for e in entries], axis=0)
                value = jnp.concatenate([value_ref[e] for e in entries], axis=0)
                s = dot(key, query_own[unit, i], NT)
                s = jnp.concatenate([s[c * BLK : (c + 1) * BLK] * SCALE2 + bias[c] for c in range(CHUNK)], axis=0)
                keys.append(key)
                scores.append(s)
                grads.append(dot(value, grad_own[unit, i], NT) - delta_all[unit, member, i])
            results = []
            for n, row in enumerate(rows):
                before = peak[row]
                top = jnp.maximum(before, jnp.max(scores[n], axis=0, keepdims=True))
                probs = jnp.exp2(scores[n] - top)
                terms = (probs * grads[n]).astype(jnp.bfloat16)
                results.append((top, jnp.exp2(before - top), jnp.sum(probs, axis=0, keepdims=True), dot(keys[n], terms, TN)))
            for n, row in enumerate(rows):
                top, shrink, summed, product = results[n]
                peak[row] = top
                total[row] = total[row] * shrink + summed
                acc[row] = acc[row] * shrink + product
        return carry

    lax.fori_loop(0, turns(table, range(ROWS)), step, 0)
    first = place()[1] == 0
    for i in range(NBLK):
        done = []
        for unit in range(2):
            row = unit * NBLK + i
            lse_ref[unit, i] = peak[row] + jnp.log2(total[row])
            done.append((acc[row] * (SCALE / total[row])).T.astype(jnp.bfloat16))
        kept_ref[i] = jnp.where(first, done[0], done[1])
        sent_ref[i] = jnp.where(first, done[1], done[0])


def flat(array):
    return array.reshape((ENTRIES,) + array.shape[3:])


def query_pass(table, query_own, grad_own, delta, key, value, peak, total, acc):
    return pl.pallas_call(
        query_kernel,
        out_shape=(
            jax.ShapeDtypeStruct(OWN[1:], jnp.bfloat16),
            jax.ShapeDtypeStruct(OWN[1:], jnp.bfloat16),
            jax.ShapeDtypeStruct((2, NBLK, 1, BLK), jnp.float32),
        ),
        in_specs=[SMEM] + [VMEM] * 8,
        out_specs=(VMEM,) * 3,
        scratch_shapes=[
            pltpu.VMEM((ROWS, 1, BLK), jnp.float32),
            pltpu.VMEM((ROWS, 1, BLK), jnp.float32),
            pltpu.VMEM((ROWS, HEAD_DIM, BLK), jnp.float32),
        ],
        compiler_params=pltpu.CompilerParams(vmem_limit_bytes=LIMIT),
        cost_estimate=pl.CostEstimate(flops=4_000_000_000, bytes_accessed=8 << 20, transcendentals=1 << 21),
        name="query_pass",
    )(table, query_own, grad_own, delta, flat(key), flat(value), peak, total, acc)


def diagonal(unit, member, query_own, grad_own, key_all, value_all, delta_at, lse_at, key_acc, value_acc):
    query = query_own[unit].reshape(NBLK * BLK, HEAD_DIM)
    grad = grad_own[unit].reshape(NBLK * BLK, HEAD_DIM)
    delta = jnp.concatenate([delta_at(unit, i) for i in range(NBLK)], axis=1)
    lse = jnp.concatenate([lse_at(unit, i) for i in range(NBLK)], axis=1)
    span = WIDE // BLK
    for u in range(0, NBLK, span):
        key = key_all[unit, member, u : u + span].reshape(WIDE, HEAD_DIM)
        value = value_all[unit, member, u : u + span].reshape(WIDE, HEAD_DIM)
        probs = jnp.exp2(dot(key, query, NT) * SCALE2 - lse)
        terms = (probs * (dot(value, grad, NT) - delta)).astype(jnp.bfloat16)
        value_part = dot(probs.astype(jnp.bfloat16), grad)
        key_part = dot(terms, query)
        for s in range(span):
            rows = slice(s * BLK, (s + 1) * BLK)
            value_acc[u + s] = value_part[rows]
            key_acc[u + s] = key_part[rows]


def share_kernel(lse_own, delta_all, query_own, grad_own, key_all, value_all, from_down, from_up, grad_part, lse_all, grad_all,
                 key_acc, value_acc, send, recv, send2, recv2, load):
    ring = Ring()
    member = ring.member

    barrier = pltpu.get_barrier_semaphore()
    for step in range(1, GROUP):
        slot = (member + step) % GROUP
        pl.semaphore_signal(barrier, inc=1, device_id=ring.device(slot), device_id_type=MESH)
    pl.semaphore_wait(barrier, GROUP - 1)
    pending = []

    def push(number, part, target, slot):
        pending.append(remote(part, target, send2.at[number], recv2.at[number], ring.device(slot)))

    push(0, grad_part.at[0, ring.down], grad_all.at[0, ring.down], ring.up)
    push(1, from_up, grad_all.at[1, ring.up], ring.down)
    push(2, from_down, grad_all.at[1, ring.down], ring.twin)
    push(3, from_up, grad_all.at[1, ring.up], ring.twin)
    for step in range(1, GROUP):
        device = ring.device((member + step) % GROUP)
        pending.append(remote(lse_own, lse_all.at[:, member], send.at[step], recv.at[step], device))


    held = [(lse_own, lse_all.at[:, member]), (from_down, grad_all.at[1, ring.down]), (from_up, grad_all.at[1, ring.up])]
    for slot in (ring.member, ring.twin):
        held.append((grad_part.at[:, slot], grad_all.at[:, slot]))
    for slot in (ring.down, ring.up, ring.twin_down, ring.twin_up):
        held.append((grad_part.at[0, slot], grad_all.at[0, slot]))
    loads = [pltpu.make_async_copy(part, target, load.at[n]) for n, (part, target) in enumerate(held)]
    for copy in loads:
        copy.start()

    diagonal(1 - ring.half, member, query_own, grad_own, key_all, value_all,
             lambda unit, i: delta_all[unit, member, i], lambda unit, i: lse_own[unit, i], key_acc, value_acc)

    far = (grad_all.at[0, ring.far], grad_all.at[1, ring.far])
    for n in range(2):
        arrived(far[n], recv2.at[n])
        push(4 + n, far[n], far[n], ring.twin)
    for copy in loads:
        copy.wait()
    for step in range(1, GROUP):
        arrived(lse_own, recv.at[step])
    arrived(grad_all.at[1, ring.twin_down], recv2.at[2])
    arrived(grad_all.at[1, ring.twin_up], recv2.at[3])
    arrived(grad_all.at[0, ring.twin_far], recv2.at[4])
    arrived(grad_all.at[1, ring.twin_far], recv2.at[5])
    for copy in pending:
        copy.wait_send()


def share_totals(lse_own, delta, query_own, grad_own, key, value, from_down, from_up, grad):
    return pl.pallas_call(
        share_kernel,
        out_shape=(
            jax.ShapeDtypeStruct(STATS, jnp.float32),
            jax.ShapeDtypeStruct(WHOLE, jnp.bfloat16),
            jax.ShapeDtypeStruct((NBLK, BLK, HEAD_DIM), jnp.float32),
            jax.ShapeDtypeStruct((NBLK, BLK, HEAD_DIM), jnp.float32),
        ),
        in_specs=[VMEM] * 8 + [ANY],
        out_specs=(VMEM,) * 4,
        scratch_shapes=[
            pltpu.SemaphoreType.DMA((GROUP,)),
            pltpu.SemaphoreType.DMA((GROUP,)),
            pltpu.SemaphoreType.DMA((6,)),
            pltpu.SemaphoreType.DMA((6,)),
            pltpu.SemaphoreType.DMA((9,)),
        ],
        compiler_params=pltpu.CompilerParams(collective_id=1, has_side_effects=True, vmem_limit_bytes=LIMIT),
        name="share_totals",
    )(lse_own, delta, query_own, grad_own, key, value, from_down, from_up, grad)


def key_kernel(blocks, table, key_all, value_all, delta_ref, lse_ref, query_ref, grad_ref, first_in, second_in, out_ref,
               key_acc, value_acc):
    _, half, member = place()
    other = len(blocks) < NBLK
    unit = 1 - half if other else half
    base = unit * NBLK
    if other:
        for u in blocks:
            key_acc[u] = first_in[u]
            value_acc[u] = second_in[u]
    else:
        own = (unit * GROUP + member) * NBLK
        diagonal(unit, member, first_in, second_in, key_all, value_all,
                 lambda unit, i: delta_ref[own + i], lambda unit, i: lse_ref[own + i], key_acc, value_acc)

    def step(turn, carry):
        for first in blocks[::PAIR]:
            pair = range(first, first + PAIR)
            loads, results = [], []
            for u in pair:
                row = base + u
                slots = [turn * CHUNK + c for c in range(CHUNK)]
                entries = [table[row, slot] for slot in slots]
                bias = [jnp.where(slot < table[row, COUNT_AT], 0.0, FAR) for slot in slots]
                query = jnp.concatenate([query_ref[e] for e in entries], axis=0)
                grad = jnp.concatenate([grad_ref[e] for e in entries], axis=0)
                lse = jnp.concatenate([lse_ref[e] + b for e, b in zip(entries, bias)], axis=1)
                delta = jnp.concatenate([delta_ref[e] for e in entries], axis=1)
                scores = dot(key_all[unit, member, u], query, NT)
                grads = dot(value_all[unit, member, u], grad, NT)
                loads.append((query, grad, lse, delta, scores, grads))
            for query, grad, lse, delta, scores, grads in loads:
                probs = jnp.exp2(scores * SCALE2 - lse)
                terms = (probs * (grads - delta)).astype(jnp.bfloat16)
                results.append((dot(probs.astype(jnp.bfloat16), grad), dot(terms, query)))
            for n, u in enumerate(pair):
                value_acc[u] += results[n][0]
                key_acc[u] += results[n][1]
        return carry

    lax.fori_loop(0, turns(table, [base + u for u in blocks]), step, 0)
    for n, u in enumerate(blocks):
        out_ref[0, n] = (key_acc[u] * SCALE).astype(jnp.bfloat16)
        out_ref[1, n] = value_acc[u].astype(jnp.bfloat16)


def key_pass(blocks, table, key, value, delta, lse, query, grad, first, second):
    def kernel(*refs):
        key_kernel(blocks, *refs)

    return pl.pallas_call(
        kernel,
        out_shape=jax.ShapeDtypeStruct((2, len(blocks), BLK, HEAD_DIM), jnp.bfloat16),
        in_specs=[SMEM] + [VMEM] * 8,
        out_specs=VMEM,
        scratch_shapes=[
            pltpu.VMEM((NBLK, BLK, HEAD_DIM), jnp.float32),
            pltpu.VMEM((NBLK, BLK, HEAD_DIM), jnp.float32),
        ],
        compiler_params=pltpu.CompilerParams(vmem_limit_bytes=LIMIT),
        cost_estimate=pl.CostEstimate(flops=2_000_000_000, bytes_accessed=1 << 20, transcendentals=1 << 20),
        name="key_pass",
    )(table, key, value, flat(delta), flat(lse), flat(query), flat(grad), first, second)


def local(queries, key_states, value_states, attn_out, grad_out, frame_order, block_live):
    first = lax.axis_index("frame") < GROUP
    frame_order, first = lax.optimization_barrier((frame_order, first))
    (key, value, query, grad, delta, query_own, grad_own, peak, total, acc, by_query, by_key, grad_half) = gather_all(
        frame_order, block_live.transpose(1, 2, 0), key_states, value_states, queries, grad_out, attn_out
    )
    round_up = [(source, source // GROUP * GROUP + (source + 2) % GROUP) for source in range(2 * GROUP)]
    from_down = lax.ppermute(grad_half, "frame", round_up)
    from_up = lax.ppermute(grad_half, "frame", [(target, source) for source, target in round_up])
    dq_kept, dq_sent, lse_own = query_pass(by_query, query_own, grad_own, delta, key, value, peak, total, acc)
    swap = [(source, (source + GROUP) % (2 * GROUP)) for source in range(2 * GROUP)]

    def across(sent):
        return lax.ppermute(sent, "frame", swap)

    def join(kept, came):
        kept, came = kept.reshape(NBLK * BLK, HEAD_DIM), came.reshape(NBLK * BLK, HEAD_DIM)
        return jnp.concatenate([jnp.where(first, kept, came), jnp.where(first, came, kept)], axis=1)

    dq_came = across(dq_sent)
    lse, grad, key_acc, value_acc = share_totals(
        lse_own, delta, query_own, grad_own, key, value, from_down, from_up, grad
    )
    gathered = (by_key, key, value, delta, lse, query, grad)
    middle = NBLK // 2
    came = [
        across(key_pass(blocks, *gathered, key_acc, value_acc)) for blocks in (range(middle), range(middle, NBLK))
    ]
    came = jnp.concatenate(came, axis=1)
    kept = key_pass(range(NBLK), *gathered, query_own, grad_own)
    return join(dq_kept, dq_came), join(kept[0], came[0]), join(kept[1], came[1])


def solution(mesh):
    rows = P(("frame", "head"), None)
    out = P("frame", "head")
    return jax.shard_map(
        local,
        mesh=mesh,
        in_specs=(rows, rows, rows, rows, rows, P(), P()),
        out_specs=(out, out, out),
        check_vma=False,
    )
```
